32 devices in a mesh: ctx: 8 (over y, x, core), head: 4 (over z).
Axes of the slice: x: 2, y: 2, z: 4, core: 2. Of those that a mesh axis runs over, the one named last changes fastest.
Arguments:
- queries: bfloat16 [8192, 8, 128], P(('ctx', 'head')), may hold values from -4.5 to 4.5
- keys_in: bfloat16 [8192, 8, 128], P(('ctx', 'head')), may hold values from -4.5 to 4.5
- values: bfloat16 [8192, 8, 128], P(('ctx', 'head')), may hold values from -6 to 6
- grad_out: bfloat16 [8192, 8, 128], P(('ctx', 'head')), may hold values from -6 to 6
- slopes: float32 [8], replicated, may hold values from 0.00024414062 to 0.03125
- doc_lengths: int32 [16], replicated, may hold values from 1 to 1024, 8192 in all
Outputs:
- grad_query: bfloat16 [8192, 8, 128], P(('ctx', 'head'))
- grad_key: bfloat16 [8192, 8, 128], P(('ctx', 'head'))
- grad_value: bfloat16 [8192, 8, 128], P(('ctx', 'head'))
The draws below stay inside these ranges and needn't reach their ends.
Inputs may be any that keep to these rules, and one draw needn't show every extreme that they name: `doc_lengths`: the 16 lengths sum to 8192, and the longest is exactly 1024.
All inputs are finite; a program needn't handle non-finite values.
Results may differ from the reference program's by a relative error of at most 0.0075.
Values may be sent and summed in bfloat16 or wider, within the bound.
A program may use at most 64 MiB of HBM per device.

```python
import math
import jax
import jax.numpy as jnp
import numpy as np
from jax import lax

HD = 128
HEADS = 8
DOCS = 16
TOK_DEV = 1024
SEQ = 8192
DOC_MAX = 1024
REACH = 1


def drawn_draw(key):
    return jnp.clip(jax.random.normal(jax.random.fold_in(key, 6), (SEQ, HEADS, HD), jnp.float32), -4.5, 4.5)


def draw_queries(key, part):
    drawn = drawn_draw(jax.random.fold_in(key, 11))
    return drawn.astype(jnp.bfloat16)


def draw_keys_in(key, part):
    drawn = drawn_draw(jax.random.fold_in(key, 13))
    return drawn.astype(jnp.bfloat16)


def block_levels(own_key, dims, pieces, smallest, top_value):
    gain = 1.0
    for dim, blocks in pieces:
        steps = jax.random.uniform(jax.random.fold_in(jax.random.fold_in(own_key, 6), dim), (blocks,), jnp.float32, smallest / len(pieces), top_value / len(pieces))
        gain = gain * jnp.repeat(jnp.exp(steps), dims[dim] // blocks).reshape((-1,) + (1,) * (len(dims) - 1 - dim))
    return gain


def length_profile(number_of, total, reach, skew):
    weights = [(1 << 20) // math.isqrt(grade ** skew) + 1 for grade in range(2, number_of + 1)]
    surplus, holding = total - reach - (number_of - 1), [1] * (number_of - 1)
    while surplus > 0:
        movable = [i for i in range(number_of - 1) if holding[i] < reach]
        pool, budget = sum([weights[i] for i in movable]), surplus
        for i in movable:
            addition = min(reach - holding[i], max(1, budget * weights[i] // pool), surplus)
            holding[i] = holding[i] + addition
            surplus = surplus - addition
    return np.array([reach] + holding)


def ragged_sizes(rng, amount, total, limit, skew):
    if amount == 2:
        one = jax.random.randint(rng, (), max(1, total - limit), min(limit, total - 1) + 1)
        return jnp.stack([one, total - one])
    sizes = jnp.asarray(length_profile(amount, total, limit, skew), jnp.int32)
    twos = (amount - 1) // 2
    donor, receiver = sizes[1:1 + 2 * twos:2], sizes[2:2 + 2 * twos:2]
    room = jnp.minimum(donor - 1, limit - receiver)
    shifted = jax.random.randint(jax.random.fold_in(rng, 1), (twos,), 0, 1 << 20) % (room + 1)
    sizes = sizes.at[1:1 + 2 * twos:2].set(donor - shifted).at[2:2 + 2 * twos:2].set(receiver + shifted)
    return sizes[jax.random.permutation(jax.random.fold_in(rng, 2), amount)]


def noise(key, shape, scale, limit, shards=(), held_as=jnp.bfloat16):
    drawn = jax.random.normal(key, shape, jnp.float32) * scale
    if len(shards) > 0:
        drawn = block_levels(key, shape, shards, -0.22, 0.18) * drawn
    return jnp.clip(drawn, min=-limit, max=limit).astype(held_as)


def setup_inputs(seed: int = 0) -> dict:
    splits = jax.random.split(jax.random.key(seed), 7)
    queries = draw_queries(jax.random.fold_in(splits[6], 71), 0)
    keys_in = draw_keys_in(jax.random.fold_in(splits[6], 71), 0)
    values = noise(splits[2], (SEQ, HEADS, HD), 1.0, 6.0, ((0, 32),))
    grad_out = noise(splits[3], (SEQ, HEADS, HD), 1.0, 6.0, ((0, 32),))
    slopes = jnp.clip(jnp.exp(jax.random.uniform(splits[4], (HEADS,), jnp.float32, math.log(0.00024414062), math.log(0.03125))), 0.00024414062, 0.03125)
    doc_lengths = ragged_sizes(splits[5], DOCS, SEQ, DOC_MAX, 2).astype(jnp.int32)
    return dict(queries=queries, keys_in=keys_in, values=values, grad_out=grad_out, slopes=slopes, doc_lengths=doc_lengths)


def reference(queries, keys_in, values, grad_out, slopes, doc_lengths):
    inv_scale = 1.0 / math.sqrt(HD)
    window = (REACH + 1) * TOK_DEV
    doc_ends = jnp.cumsum(doc_lengths).astype(jnp.int32)
    doc_starts = (doc_ends - doc_lengths).astype(jnp.int32)
    positions = jnp.arange(SEQ, dtype=jnp.int32)
    row_starts = lax.optimization_barrier(jnp.max(jnp.where(doc_starts[None, :] <= positions[:, None], doc_starts[None, :], 0), axis=1)).astype(jnp.int32)
    padding = jnp.zeros((REACH * TOK_DEV, HEADS, HD), keys_in.dtype)
    keys_pad = jnp.concatenate([padding, keys_in], axis=0)
    values_pad = jnp.concatenate([padding, values], axis=0)
    acc_zero = jnp.zeros((SEQ + REACH * TOK_DEV, HEADS, HD), jnp.float32)

    def block_step(carried, block_index):
        key_acc, value_acc = carried
        first_row = (block_index * TOK_DEV).astype(jnp.int32)
        q_block = lax.dynamic_slice_in_dim(queries, first_row, TOK_DEV, 0).astype(jnp.float32)
        g_block = lax.dynamic_slice_in_dim(grad_out, first_row, TOK_DEV, 0).astype(jnp.float32)
        k_window = lax.dynamic_slice_in_dim(keys_pad, first_row, window, 0).astype(jnp.float32)
        v_window = lax.dynamic_slice_in_dim(values_pad, first_row, window, 0).astype(jnp.float32)
        q_pos = first_row + jnp.arange(TOK_DEV, dtype=jnp.int32)
        k_pos = first_row - REACH * TOK_DEV + jnp.arange(window, dtype=jnp.int32)
        q_starts = lax.dynamic_slice_in_dim(row_starts, first_row, TOK_DEV, 0)
        raw = jnp.einsum('qhd,khd->hqk', q_block, k_window)
        distance = (q_pos[:, None] - k_pos[None, :]).astype(jnp.float32)
        scores = raw * inv_scale - slopes[:, None, None] * distance[None]
        allowed = ((k_pos[None, :] <= q_pos[:, None]) & (k_pos[None, :] >= q_starts[:, None]))[None]
        row_max = lax.optimization_barrier(jnp.max(jnp.where(allowed, scores, -1e+30), axis=2))
        row_sum = lax.optimization_barrier(jnp.sum(jnp.where(allowed, jnp.exp(scores - row_max[:, :, None]), 0.0), axis=2))
        log_total = row_max + jnp.log(row_sum)
        weights = jnp.where(allowed, jnp.exp(scores - log_total[:, :, None]), 0.0)
        weights_b = lax.optimization_barrier(weights.astype(jnp.bfloat16)).astype(jnp.float32)
        attn_out = jnp.einsum('hqk,khd->qhd', weights_b, v_window)
        row_delta = lax.optimization_barrier(jnp.sum(g_block * attn_out, axis=2)).T
        dweights = jnp.einsum('qhd,khd->hqk', g_block, v_window)
        dscores = weights * (dweights - row_delta[:, :, None])
        dscores_b = lax.optimization_barrier(dscores.astype(jnp.bfloat16)).astype(jnp.float32)
        grad_rows = (jnp.einsum('hqk,khd->qhd', dscores_b, k_window) * inv_scale).astype(jnp.bfloat16)
        key_term = jnp.einsum('hqk,qhd->khd', dscores_b, q_block)
        value_term = jnp.einsum('hqk,qhd->khd', weights_b, g_block)
        key_acc = lax.dynamic_update_slice_in_dim(key_acc, lax.dynamic_slice_in_dim(key_acc, first_row, window, 0) + key_term, first_row, 0)
        value_acc = lax.dynamic_update_slice_in_dim(value_acc, lax.dynamic_slice_in_dim(value_acc, first_row, window, 0) + value_term, first_row, 0)
        return ((key_acc, value_acc), grad_rows)
    (key_acc, value_acc), grad_blocks = lax.scan(block_step, (acc_zero, acc_zero), jnp.arange(SEQ // TOK_DEV, dtype=jnp.int32))
    grad_query = grad_blocks.reshape(SEQ, HEADS, HD)
    grad_key = (key_acc[REACH * TOK_DEV:] * inv_scale).astype(jnp.bfloat16)
    grad_value = value_acc[REACH * TOK_DEV:].astype(jnp.bfloat16)
    return (grad_query, grad_key, grad_value)
```

```python
from functools import partial
import math

import jax
import jax.numpy as jnp
from jax import lax
from jax.experimental import pallas as pl
from jax.experimental.pallas import tpu as pltpu
from jax.sharding import PartitionSpec as P

F32 = jnp.float32
BF16 = jnp.bfloat16
VMEM_ALL = 65208320
LOG2E = math.log2(math.e)
NT = (((1,), (1,)), ((), ()))
NN = (((1,), (0,)), ((), ()))
TN = (((0,), (0,)), ((), ()))


def repeat(count, step):
    if count <= 8:
        for n in range(count):
            step(n)
    else:

        def looped(n, carry):
            step(n)
            return carry

        lax.fori_loop(0, count, looped, 0)


def kernel(
    sizes,
    k_hbm, v_hbm, q_hbm, g_hbm, slope_hbm, doc_hbm,
    dq_hbm, dk_hbm, dv_hbm,
    k_raw, v_raw, q_raw, g_raw, k_in, v_in, q_in, g_in, dq_out, dk_out, dv_out, slope_ref, doc_ref, low_ref,
    k_all, v_all, q_all, g_all,
    s_buf, dp_buf, top, low_sum, weighted, dq_acc, dk_acc, dv_acc,
    dq_mine, dk_mine, dv_mine, dk_part, dv_part, dk_got, dv_got,
    small_sem, raw_sem, own_sem, in_send, in_recv, fwd_send, fwd_recv, back_send, back_recv, out_send, out_recv,
):
    n_head, n_ctx, reach, here, tok, rows, depth, tile = sizes
    z = lax.axis_index("head")
    c = lax.axis_index("ctx")
    past = reach * rows
    chunks = (past + tile) // tile
    inv_scale = 1.0 / math.sqrt(depth)

    def peer(off):
        other, bit = z, 1
        while bit < n_head:
            if off & bit:
                other = other + bit * (1 - 2 * lax.rem(z // bit, 2))
            bit *= 2
        return other

    offs = tuple(range(1, n_head))

    def along(off):
        return lax.rem(c + off + n_ctx, n_ctx)

    wholes = (k_hbm, v_hbm, q_hbm, g_hbm)
    raws = (k_raw, v_raw, q_raw, g_raw)

    def raw_copy(a):
        return pltpu.make_async_copy(wholes[a], raws[a], raw_sem.at[a])

    for a in range(4):
        raw_copy(a).start()
    small = (
        pltpu.make_async_copy(slope_hbm, slope_ref, small_sem.at[0]),
        pltpu.make_async_copy(doc_hbm, doc_ref, small_sem.at[1]),
    )
    for copy in small:
        copy.start()

    barrier = pltpu.get_barrier_semaphore()
    for off in range(1, n_head):
        pl.semaphore_signal(barrier, inc=1, device_id={"head": peer(off)}, device_id_type=pl.DeviceIdType.MESH)
    for off in range(1, reach + 1):
        for side in (off, -off):
            pl.semaphore_signal(barrier, inc=1, device_id={"ctx": along(side)}, device_id_type=pl.DeviceIdType.MESH)

    sources = (k_in, v_in, q_in, g_in)
    holders = (k_all, v_all, q_all, g_all)
    bases = (past, past, 0, 0)

    def own_copy(i, a):
        return pltpu.make_async_copy(
            sources[a].at[z * here + i],
            holders[a].at[i, pl.ds(pl.multiple_of(bases[a] + z * tok, tok), tok)],
            own_sem.at[i, a],
        )

    def in_copy(i, a, off):
        return pltpu.make_async_remote_copy(
            src_ref=sources[a].at[peer(off) * here + i],
            dst_ref=holders[a].at[i, pl.ds(pl.multiple_of(bases[a] + z * tok, tok), tok)],
            send_sem=in_send.at[i, a, off - 1],
            recv_sem=in_recv.at[i, a, off - 1],
            device_id={"head": peer(off)},
            device_id_type=pl.DeviceIdType.MESH,
        )

    def fwd_copy(i, a, r):
        return pltpu.make_async_remote_copy(
            src_ref=holders[a].at[i, pl.ds(past, rows)],
            dst_ref=holders[a].at[i, pl.ds((reach - r) * rows, rows)],
            send_sem=fwd_send.at[i, a, r - 1],
            recv_sem=fwd_recv.at[i, a, r - 1],
            device_id={"ctx": along(r)},
            device_id_type=pl.DeviceIdType.MESH,
        )

    parts = (dk_part, dv_part)
    gots = (dk_got, dv_got)

    def back_copy(i, a, r):
        return pltpu.make_async_remote_copy(
            src_ref=parts[a].at[i, pl.ds((reach - r) * rows, rows)],
            dst_ref=gots[a].at[i, r - 1],
            send_sem=back_send.at[i, a, r - 1],
            recv_sem=back_recv.at[i, a, r - 1],
            device_id={"ctx": along(-r)},
            device_id_type=pl.DeviceIdType.MESH,
        )

    mine = (dq_mine, dk_mine, dv_mine)
    outs = (dq_out, dk_out, dv_out)

    def out_copy(i, a, off):
        return pltpu.make_async_remote_copy(
            src_ref=mine[a].at[i, pl.ds(pl.multiple_of(peer(off) * tok, tok), tok)],
            dst_ref=outs[a].at[z * here + i],
            send_sem=out_send.at[i, a, off - 1],
            recv_sem=out_recv.at[i, a, off - 1],
            device_id={"head": peer(off)},
            device_id_type=pl.DeviceIdType.MESH,
        )

    def send_out(i, a):
        for off in offs:
            out_copy(i, a, off).start()
        outs[a][z * here + i] = mine[a][i, pl.ds(pl.multiple_of(z * tok, tok), tok)]

    def arrived(i, a):
        own_copy(i, a).wait()
        for off in range(1, n_head):
            in_copy(i, a, off).wait_recv()

    def attend(i):
        slope2 = slope_ref[z * here + i] * LOG2E
        dk_acc[...] = jnp.zeros_like(dk_acc)
        dv_acc[...] = jnp.zeros_like(dv_acc)

        def block(b, carry):
            first = pl.multiple_of(b * tile, tile)
            q = q_all[i, pl.ds(first, tile)]
            g = g_all[i, pl.ds(first, tile)]
            low = low_ref[:, pl.ds(first, tile)] + (past - first).astype(F32)
            high = past + lax.broadcasted_iota(jnp.int32, (1, tile), 1)
            high = high.astype(F32)
            spot = lax.broadcasted_iota(jnp.int32, (tile, tile), 0).astype(F32)
            top[...] = jnp.full_like(top, -1e30)
            low_sum[...] = jnp.zeros_like(low_sum)
            weighted[...] = jnp.zeros_like(weighted)
            dq_acc[...] = jnp.zeros_like(dq_acc)

            def window(n):
                return pl.ds(pl.multiple_of(first + n * tile, tile), tile)

            def held(n):
                return pl.ds(pl.multiple_of(n * tile, tile), tile)

            def score(n):
                raw = lax.dot_general(k_all[i, window(n)], q, NT, preferred_element_type=F32)
                where = spot + jnp.float32(n * tile)
                s = raw * (inv_scale * LOG2E) + slope2 * (where - past)
                s = jnp.where((where >= low) & (where <= high), s, -1e30)
                s_buf[held(n)] = s
                top[...] = jnp.maximum(top[...], jnp.max(s, axis=0, keepdims=True))

            def weigh(n):
                p = jnp.exp2(s_buf[held(n)] - top[...])
                dp = lax.dot_general(v_all[i, window(n)], g, NT, preferred_element_type=F32)
                s_buf[held(n)] = p
                dp_buf[held(n)] = dp
                low_sum[...] += jnp.sum(p, axis=0, keepdims=True)
                weighted[...] += jnp.sum(p * dp, axis=0, keepdims=True)

            repeat(chunks, score)
            repeat(chunks, weigh)
            share = 1.0 / low_sum[...]
            delta = weighted[...] * share

            def spread(n):
                w = s_buf[held(n)] * share
                ds = (w * (dp_buf[held(n)] - delta)).astype(BF16)
                dv_acc[window(n)] += lax.dot_general(w.astype(BF16), g, NN, preferred_element_type=F32)
                dk_acc[window(n)] += lax.dot_general(ds, q, NN, preferred_element_type=F32)
                dq_acc[...] += lax.dot_general(k_all[i, window(n)], ds, TN, preferred_element_type=F32)

            repeat(chunks, spread)
            dq_mine[i, pl.ds(first, tile)] = (dq_acc[...] * inv_scale).T.astype(BF16)
            return carry

        lax.fori_loop(0, rows // tile, block, 0)
        dk_part[i] = dk_acc[pl.ds(0, past)].astype(BF16)
        dv_part[i] = dv_acc[pl.ds(0, past)].astype(BF16)

    def settle(i, a, acc, scale):
        total = acc
        for r in range(1, reach + 1):
            back_copy(i, a, r).wait_recv()
            total = total + gots[a][i, r - 1].astype(F32)
        mine[1 + a][i] = (total * scale).astype(BF16)
        send_out(i, 1 + a)

    def start_head(i, a):
        for off in offs:
            in_copy(i, a, off).start()
        own_copy(i, a).start()

    def turn(source, target, count):
        if source.shape[0] == tok:
            for n in range(0, tok, count):
                target[:, n : n + count] = jnp.swapaxes(source[n : n + count], 0, 1)
        else:
            for n in range(0, tok, count):
                target[n : n + count] = jnp.swapaxes(source[:, n : n + count], 0, 1)

    step = min(64, tok)
    for a in range(4):
        raw_copy(a).wait()
        turn(raws[a], sources[a], step)
        if a == 0:
            pl.semaphore_wait(barrier, n_head - 1 + 2 * reach)
        start_head(0, a)
    for i in range(1, here):
        for a in range(4):
            start_head(i, a)

    for copy in small:
        copy.wait()
    spots = lax.broadcasted_iota(jnp.int32, (1, rows), 1) + c * rows
    start = jnp.int32(0)
    low = jnp.zeros((1, rows), jnp.int32)
    for n in range(doc_ref.shape[0]):
        low = jnp.where(spots >= start, start, low)
        start = start + doc_ref[n]
    low_ref[...] = (low - c * rows).astype(F32)

    def forward(i):
        for a in range(2):
            arrived(i, a)
            for r in range(1, reach + 1):
                fwd_copy(i, a, r).start()

    forward(0)
    for i in range(here):
        for a in (2, 3):
            arrived(i, a)
        for a in range(2):
            for r in range(1, reach + 1):
                fwd_copy(i, a, r).wait_recv()
        attend(i)
        for a in range(2):
            for r in range(1, reach + 1):
                back_copy(i, a, r).start()
        send_out(i, 0)
        if i + 1 < here:
            forward(i + 1)
        settle(i, 0, dk_acc[pl.ds(past, rows)], inv_scale)
        settle(i, 1, dv_acc[pl.ds(past, rows)], 1.0)

    results = (dq_hbm, dk_hbm, dv_hbm)

    def result_copy(a):
        return pltpu.make_async_copy(raws[a], results[a], raw_sem.at[a])

    for a in range(3):
        for i in range(here):
            for off in offs:
                out_copy(i, a, off).wait_recv()
        turn(outs[a], raws[a], step)
        result_copy(a).start()

    for i in range(here):
        for off in offs:
            for a in range(4):
                in_copy(i, a, off).wait_send()
            for a in range(3):
                out_copy(i, a, off).wait_send()
        for a in range(2):
            for r in range(1, reach + 1):
                fwd_copy(i, a, r).wait_send()
                back_copy(i, a, r).wait_send()
    for a in range(3):
        result_copy(a).wait()


def chain_kernel(
    sizes,
    k_hbm, v_hbm, q_hbm, g_hbm, slope_hbm, doc_hbm,
    dq_hbm, dk_hbm, dv_hbm,
    k_raw, v_raw, q_raw, g_raw, k_in, v_in, q_in, g_in, dq_out, dk_out, dv_out, slope_ref, doc_ref, low_ref,
    k_all, v_all, q_all, g_all,
    p_buf, dp_buf, top, stat, stat_got, both, dq_acc, dk_acc, dv_acc, dq_rows,
    dq_own, dq_next, dq_far, got_next, got_far, got_side, dq_pair, dk_pair, dv_pair, got_pair,
    small_sem, raw_sem, own_sem, in_send, in_recv, near_send, near_recv, far_send, far_recv,
    stat_send, stat_recv, next_send, next_recv, side_recv, back_send, back_recv, pair_send, pair_recv,
):
    n_ctx, mine, tok, depth = sizes
    z = lax.axis_index("head")
    c = lax.axis_index("ctx")
    side = z // 2
    half = lax.rem(z, 2)
    rest = 1 - half
    chunk = 2 * tok
    span = 3 * chunk
    first_key = (2 * c + side) * chunk
    inner = lax.rem(side + half, 2) == 1
    outer = lax.rem(side + half, 2) == 0
    inv_scale = 1.0 / math.sqrt(depth)

    before, after = lax.rem(c - 1 + n_ctx, n_ctx), lax.rem(c + 1, n_ctx)
    c_less = lax.rem(c - (1 - side) + n_ctx, n_ctx)
    c_more = lax.rem(c + side, n_ctx)
    across = z + 2 - 4 * side
    mirror = 3 - z
    twin = {"head": z + 1 - 2 * half}
    less_one, more_one = {"ctx": c_less, "head": across}, {"ctx": c_more, "head": across}
    less_mirror, more_mirror = {"ctx": c_less, "head": mirror}, {"ctx": c_more, "head": mirror}
    less_two, more_two = {"ctx": before}, {"ctx": after}

    def remote(src, dst, send, recv, device):
        return pltpu.make_async_remote_copy(
            src_ref=src, dst_ref=dst, send_sem=send, recv_sem=recv,
            device_id=device, device_id_type=pl.DeviceIdType.MESH,
        )

    wholes = (k_hbm, v_hbm, q_hbm, g_hbm)
    raws = (k_raw, v_raw, q_raw, g_raw)
    sources = (k_in, v_in, q_in, g_in)
    holders = (k_all, v_all, q_all, g_all)

    def raw_copy(a):
        return pltpu.make_async_copy(wholes[a], raws[a], raw_sem.at[a])

    for a in (2, 3, 0, 1):
        raw_copy(a).start()
    small = (
        pltpu.make_async_copy(slope_hbm, slope_ref, small_sem.at[0]),
        pltpu.make_async_copy(doc_hbm, doc_ref, small_sem.at[1]),
    )
    for copy in small:
        copy.start()

    barrier = pltpu.get_barrier_semaphore()
    peers = (twin, less_one, more_one, less_mirror, more_mirror, less_two, more_two)
    for device in peers:
        pl.semaphore_signal(barrier, inc=1, device_id=device, device_id_type=pl.DeviceIdType.MESH)

    def block(base, which):
        return pl.ds(pl.multiple_of(base + which * tok, tok), tok)

    def own_copy(i, a):
        return pltpu.make_async_copy(sources[a].at[half * mine + i], holders[a].at[i, block(0, half)], own_sem.at[i, a])

    def in_copy(i, a):
        return remote(
            sources[a].at[rest * mine + i], holders[a].at[i, block(0, half)], in_send.at[i, a], in_recv.at[i, a], twin
        )

    def near_own(i, a):
        return remote(
            sources[a].at[half * mine + i], holders[a].at[i, block(chunk, half)],
            near_send.at[i, a - 2, 0], near_recv.at[i, a - 2, half], less_one,
        )

    def near_other(i, a):
        return remote(
            sources[a].at[rest * mine + i], holders[a].at[i, block(chunk, half)],
            near_send.at[i, a - 2, 1], near_recv.at[i, a - 2, half], less_mirror,
        )

    def near_relay(i, a):
        return remote(
            holders[a].at[i, block(0, rest)], holders[a].at[i, block(chunk, rest)],
            near_send.at[i, a - 2, 2], near_recv.at[i, a - 2, rest], less_one,
        )

    def far_copy(i, a):
        return remote(
            holders[a].at[i, pl.ds(0, chunk)], holders[a].at[i, pl.ds(2 * chunk, chunk)],
            far_send.at[i, a - 2], far_recv.at[i, a - 2], less_two,
        )

    routes = (
        (0, less_one, 1, 0),
        (0, less_two, 2, 0),
        (1, more_one, 0, 0),
        (1, less_one, 2, 1),
        (2, more_two, 0, 1),
        (2, more_one, 1, 1),
    )

    def stat_copy(i, m):
        slot, device, there, place = routes[m]
        return remote(
            stat.at[i, slot], stat_got.at[i, there, place], stat_send.at[i, m], stat_recv.at[i, there, place], device
        )

    def next_own(i):
        return remote(
            dq_next.at[i, block(0, half)], got_next.at[i], next_send.at[i, 0], next_recv.at[i], more_one
        )

    def next_side(i):
        kind = lax.rem(side + half + 1, 2)
        device = {"ctx": c_more, "head": 2 - side}
        return remote(
            dq_next.at[i, block(0, rest)], got_side.at[kind, i], next_send.at[i, 1], side_recv.at[kind, i], device
        )

    def back_copy(i):
        return remote(dq_far.at[i], got_far.at[i], back_send.at[i], back_recv.at[i], more_two)

    pairs = (dq_pair, dk_pair, dv_pair)
    pair_targets = (None, dk_out, dv_out)

    def pair_copy(i, a):
        target = got_pair.at[i] if a == 0 else pair_targets[a].at[half * mine + i]
        return remote(pairs[a].at[i], target, pair_send.at[i, a], pair_recv.at[i, a], twin)

    def pair_wait(i, a):
        target = got_pair.at[i] if a == 0 else pair_targets[a].at[rest * mine + i]
        remote(pairs[a].at[i], target, pair_send.at[i, a], pair_recv.at[i, a], twin).wait_recv()

    step = min(64, tok)

    def turn(source, target):
        if source.shape[0] == tok:
            for n in range(0, tok, step):
                target[:, n : n + step] = jnp.swapaxes(source[n : n + step], 0, 1)
        else:
            for n in range(0, tok, step):
                target[n : n + step] = jnp.swapaxes(source[:, n : n + step], 0, 1)

    def open_head(i, a):
        in_copy(i, a).start()
        own_copy(i, a).start()
        if a >= 2:
            near_own(i, a).start()

            @pl.when(inner)
            def _():
                near_other(i, a).start()

    def relay(i):
        for a in (2, 3):
            own_copy(i, a).wait()
            in_copy(i, a).wait_recv()
            far_copy(i, a).start()

            @pl.when(inner)
            def _():
                near_relay(i, a).start()

    def arrived(i):
        for a in (0, 1):
            own_copy(i, a).wait()
            in_copy(i, a).wait_recv()
        for a in (2, 3):
            far_copy(i, a).wait_recv()
            near_own(i, a).wait_recv()
            near_relay(i, a).wait_recv()

    def tile_rows(t):
        return pl.ds(pl.multiple_of(t * tok, tok), tok)

    def gather(i, slot_of):
        slope2 = slope_ref[half * mine + i] * LOG2E

        def slot_step(slot, carry):
            for u in range(2):
                t = 2 * slot + u
                q = q_all[i, tile_rows(t)]
                g = g_all[i, tile_rows(t)]
                low = low_ref[:, tile_rows(t)]
                first = (t * tok).astype(F32)
                high = lax.broadcasted_iota(jnp.int32, (1, tok), 1).astype(F32) + first
                spot = lax.broadcasted_iota(jnp.int32, (tok, tok), 0).astype(F32)
                best = jnp.full((1, tok), -1e30, F32)
                for b in range(2):
                    raw = lax.dot_general(k_all[i, b * tok : (b + 1) * tok], q, NT, preferred_element_type=F32)
                    where = spot + jnp.float32(b * tok)
                    s = raw * (inv_scale * LOG2E) + slope2 * (where - first)
                    s = jnp.where((where >= low) & (where <= high), s, -1e30)
                    p_buf[slot_of, t, b] = s
                    best = jnp.maximum(best, jnp.max(s, axis=0, keepdims=True))
                total = jnp.zeros((1, tok), F32)
                weighted = jnp.zeros((1, tok), F32)
                for b in range(2):
                    p = jnp.exp2(p_buf[slot_of, t, b] - best)
                    dp = lax.dot_general(v_all[i, b * tok : (b + 1) * tok], g, NT, preferred_element_type=F32)
                    p_buf[slot_of, t, b] = p
                    dp_buf[slot_of, t, b] = dp
                    total = total + jnp.sum(p, axis=0, keepdims=True)
                    weighted = weighted + jnp.sum(p * dp, axis=0, keepdims=True)
                top[slot_of, t] = best
                level = best + jnp.log2(total)
                share = weighted / total
                for r in range(lanes):
                    row = u * lanes + r
                    part = slice(r * depth, (r + 1) * depth)
                    stat[i, slot, row : row + 1] = level[:, part]
                    stat[i, slot, 2 * lanes + row : 2 * lanes + row + 1] = share[:, part]
            return carry

        lax.fori_loop(0, 3, slot_step, 0)
        for m in range(6):
            stat_copy(i, m).start()

    lanes = tok // depth

    def spread(i, slot_of):
        for slot in range(3):
            for place in range(2):
                remote(
                    stat.at[i, slot], stat_got.at[i, slot, place], stat_send.at[i, 0], stat_recv.at[i, slot, place], twin
                ).wait_recv()
            found = (stat[i, slot], stat_got[i, slot, 0], stat_got[i, slot, 1])
            levels = [x[: 2 * lanes] for x in found]
            shares = [x[2 * lanes :] for x in found]
            peak = jnp.maximum(jnp.maximum(levels[0], levels[1]), levels[2])
            full = peak + jnp.log2(sum(jnp.exp2(x - peak) for x in levels))
            delta = sum(jnp.exp2(x - full) * y for x, y in zip(levels, shares))
            for u in range(2):
                for r in range(lanes):
                    row = u * lanes + r
                    part = slice(r * depth, (r + 1) * depth)
                    both[0, 2 * slot + u, :, part] = full[row : row + 1]
                    both[1, 2 * slot + u, :, part] = delta[row : row + 1]
        dk_acc[...] = jnp.zeros_like(dk_acc)
        dv_acc[...] = jnp.zeros_like(dv_acc)

        def tile_step(t, carry):
            q = q_all[i, tile_rows(t)]
            g = g_all[i, tile_rows(t)]
            share = jnp.exp2(top[slot_of, t] - both[0, t])
            delta = both[1, t]
            for b in range(2):
                rows = slice(b * tok, (b + 1) * tok)
                w = p_buf[slot_of, t, b] * share
                ds = (w * (dp_buf[slot_of, t, b] - delta)).astype(BF16)
                dv_acc[rows] += lax.dot_general(w.astype(BF16), g, NN, preferred_element_type=F32)
                dk_acc[rows] += lax.dot_general(ds, q, NN, preferred_element_type=F32)
                part = lax.dot_general(k_all[i, rows], ds, TN, preferred_element_type=F32)
                if b == 0:
                    dq_acc[...] = part
                else:
                    dq_acc[...] += part
            dq_rows[tile_rows(t)] = (dq_acc[...] * inv_scale).T
            return carry

        lax.fori_loop(0, 6, tile_step, 0)
        dq_next[i] = dq_rows[chunk : 2 * chunk].astype(BF16)
        next_side(i).start()
        next_own(i).start()
        dq_far[i] = dq_rows[2 * chunk : 3 * chunk].astype(BF16)
        back_copy(i).start()
        dq_own[i] = dq_rows[0:chunk]
        dk_pair[i] = (dk_acc[block(0, rest)] * inv_scale).astype(BF16)
        pair_copy(i, 1).start()
        dv_pair[i] = dv_acc[block(0, rest)].astype(BF16)
        pair_copy(i, 2).start()
        dk_out[half * mine + i] = (dk_acc[block(0, half)] * inv_scale).astype(BF16)
        dv_out[half * mine + i] = dv_acc[block(0, half)].astype(BF16)

    def settle(i):
        back_copy(i).wait_recv()

        @pl.when(inner)
        def _():
            remote(dq_pair.at[i], got_side.at[1, i], next_send.at[i, 1], side_recv.at[1, i], twin).wait_recv()

        dq_pair[i] = (
            dq_own[i, block(0, rest)] + got_far[i, block(0, rest)].astype(F32) + got_side[1, i].astype(F32)
        ).astype(BF16)
        pair_copy(i, 0).start()
        next_own(i).wait_recv()
        dq_out[half * mine + i] = (
            dq_own[i, block(0, half)] + got_far[i, block(0, half)].astype(F32) + got_next[i].astype(F32)
        ).astype(BF16)

    def close(i):
        pair_wait(i, 0)

        @pl.when(inner)
        def _():
            remote(dq_pair.at[i], got_side.at[0, i], next_send.at[i, 1], side_recv.at[0, i], twin).wait_recv()

        dq_out[rest * mine + i] = (got_pair[i].astype(F32) + got_side[0, i].astype(F32)).astype(BF16)

    for a in (2, 3, 0, 1):
        raw_copy(a).wait()
        turn(raws[a], sources[a])
        if a == 2:
            pl.semaphore_wait(barrier, len(peers))
        open_head(0, a)
    for a in (2, 3, 0, 1):
        if mine > 1:
            open_head(1, a)

    @pl.when(outer)
    def _():
        got_side[...] = jnp.zeros_like(got_side)

    for copy in small:
        copy.wait()
    spots = lax.broadcasted_iota(jnp.int32, (1, span), 1) + first_key
    start = jnp.int32(0)
    low = jnp.zeros((1, span), jnp.int32)
    for n in range(doc_ref.shape[0]):
        low = jnp.where(spots >= start, start, low)
        start = start + doc_ref[n]
    low = jnp.where(spots >= start, spots + 1, low)
    low_ref[...] = (low - first_key).astype(F32)

    relay(0)
    for i in range(mine):
        if i + 1 < mine:
            relay(i + 1)
        if i + 2 < mine:
            for a in (2, 3, 0, 1):
                open_head(i + 2, a)
        arrived(i)
        gather(i, i % 2)
        if i >= 1:
            spread(i - 1, (i - 1) % 2)
        if i >= 2:
            settle(i - 2)
    spread(mine - 1, (mine - 1) % 2)
    for i in range(max(0, mine - 2), mine):
        settle(i)

    results = (dq_hbm, dk_hbm, dv_hbm)
    outs = (dq_out, dk_out, dv_out)

    def result_copy(a):
        return pltpu.make_async_copy(raws[a], results[a], raw_sem.at[a])

    for a in (1, 2):
        for i in range(mine):
            pair_wait(i, a)
        turn(outs[a], raws[a])
        result_copy(a).start()
    for i in range(mine):
        close(i)
    turn(outs[0], raws[0])
    result_copy(0).start()

    for i in range(mine):
        for a in range(4):
            in_copy(i, a).wait_send()
        for a in (2, 3):
            near_own(i, a).wait_send()
            far_copy(i, a).wait_send()
        for m in range(6):
            stat_copy(i, m).wait_send()
        next_own(i).wait_send()
        next_side(i).wait_send()
        back_copy(i).wait_send()
        for a in range(3):
            pair_copy(i, a).wait_send()

    @pl.when(inner)
    def _():
        for i in range(mine):
            for a in (2, 3):
                near_other(i, a).wait_send()
                near_relay(i, a).wait_send()

    for a in range(3):
        result_copy(a).wait()


def chain_call(n_ctx, tok, heads, depth, slots, docs):
    mine = heads // 2
    chunk = 2 * tok
    away = pl.BlockSpec(memory_space=pl.ANY)
    dma = pltpu.SemaphoreType.DMA
    out = jax.ShapeDtypeStruct((tok, heads, depth), BF16)
    pairs = mine * 6 * chunk * tok
    return pl.pallas_call(
        partial(chain_kernel, (n_ctx, mine, tok, depth)),
        out_shape=(out, out, out),
        in_specs=[away] * 6,
        out_specs=(away,) * 3,
        scratch_shapes=[pltpu.VMEM((tok, heads, depth), BF16)] * 4
        + [pltpu.VMEM((heads, tok, depth), BF16)] * 7
        + [
            pltpu.SMEM(slots, F32),
            pltpu.SMEM(docs, jnp.int32),
            pltpu.VMEM((1, 3 * chunk), F32),
            pltpu.VMEM((mine, chunk, depth), BF16),
            pltpu.VMEM((mine, chunk, depth), BF16),
            pltpu.VMEM((mine, 3 * chunk, depth), BF16),
            pltpu.VMEM((mine, 3 * chunk, depth), BF16),
            pltpu.VMEM((2, 6, 2, tok, tok), F32),
            pltpu.VMEM((2, 6, 2, tok, tok), F32),
            pltpu.VMEM((2, 6, 1, tok), F32),
            pltpu.VMEM((mine, 3, 4 * tok // depth, depth), F32),
            pltpu.VMEM((mine, 3, 2, 4 * tok // depth, depth), F32),
            pltpu.VMEM((2, 6, 1, tok), F32),
            pltpu.VMEM((depth, tok), F32),
            pltpu.VMEM((chunk, depth), F32),
            pltpu.VMEM((chunk, depth), F32),
            pltpu.VMEM((3 * chunk, depth), F32),
            pltpu.VMEM((mine, chunk, depth), F32),
            pltpu.VMEM((mine, chunk, depth), BF16),
            pltpu.VMEM((mine, chunk, depth), BF16),
            pltpu.VMEM((mine, tok, depth), BF16),
            pltpu.VMEM((mine, chunk, depth), BF16),
            pltpu.VMEM((2, mine, tok, depth), BF16),
            pltpu.VMEM((mine, tok, depth), BF16),
            pltpu.VMEM((mine, tok, depth), BF16),
            pltpu.VMEM((mine, tok, depth), BF16),
            pltpu.VMEM((mine, tok, depth), BF16),
            dma((2,)),
            dma((4,)),
            dma((mine, 4)),
            dma((mine, 4)),
            dma((mine, 4)),
            dma((mine, 2, 3)),
            dma((mine, 2, 2)),
            dma((mine, 2)),
            dma((mine, 2)),
            dma((mine, 6)),
            dma((mine, 3, 2)),
            dma((mine, 2)),
            dma((mine,)),
            dma((2, mine)),
            dma((mine,)),
            dma((mine,)),
            dma((mine, 3)),
            dma((mine, 3)),
        ],
        compiler_params=pltpu.CompilerParams(
            collective_id=1, has_side_effects=True, vmem_limit_bytes=VMEM_ALL
        ),
        cost_estimate=pl.CostEstimate(
            flops=10 * pairs * depth, bytes_accessed=14 * heads * tok * depth, transcendentals=pairs
        ),
    )


def hand_over(a_in, b_in, c_in, a_out, b_out, c_out, a_buf, b_buf, c_buf, in_sem, out_sem):
    bufs = (a_buf, b_buf, c_buf)
    ins = [pltpu.make_async_copy(x, bufs[n], in_sem.at[n]) for n, x in enumerate((a_in, b_in, c_in))]
    outs = [pltpu.make_async_copy(bufs[n], x, out_sem.at[n]) for n, x in enumerate((a_out, b_out, c_out))]
    for copy in ins:
        copy.start()
    for arrive, leave in zip(ins, outs):
        arrive.wait()
        leave.start()
    for copy in outs:
        copy.wait()


def body(queries, keys_in, values, grad_out, slopes, doc_lengths):
    n_head = lax.axis_size("head")
    n_ctx = lax.axis_size("ctx")
    tok, heads, depth = queries.shape
    here = heads // n_head
    rows = tok * n_head
    span = min(16384, rows * n_ctx // 8)
    reach = span // rows
    past = reach * rows
    tile = min(256, rows)
    sizes = (n_head, n_ctx, reach, here, tok, rows, depth, tile)
    away = pl.BlockSpec(memory_space=pl.ANY)
    dma = pltpu.SemaphoreType.DMA
    out = jax.ShapeDtypeStruct((tok, heads, depth), BF16)
    swapped = pltpu.VMEM((heads, tok, depth), BF16)
    window = past + tile
    pairs = rows * window * here
    call = pl.pallas_call(
        partial(kernel, sizes),
        out_shape=(out, out, out),
        in_specs=[away] * 6,
        out_specs=(away,) * 3,
        scratch_shapes=[pltpu.VMEM((tok, heads, depth), BF16)] * 4
        + [swapped] * 7
        + [
            pltpu.SMEM(slopes.shape, F32),
            pltpu.SMEM(doc_lengths.shape, jnp.int32),
            pltpu.VMEM((1, rows), F32),
            pltpu.VMEM((here, past + rows, depth), BF16),
            pltpu.VMEM((here, past + rows, depth), BF16),
            pltpu.VMEM((here, rows, depth), BF16),
            pltpu.VMEM((here, rows, depth), BF16),
            pltpu.VMEM((window, tile), F32),
            pltpu.VMEM((window, tile), F32),
            pltpu.VMEM((1, tile), F32),
            pltpu.VMEM((1, tile), F32),
            pltpu.VMEM((1, tile), F32),
            pltpu.VMEM((depth, tile), F32),
            pltpu.VMEM((past + rows, depth), F32),
            pltpu.VMEM((past + rows, depth), F32),
            pltpu.VMEM((here, rows, depth), BF16),
            pltpu.VMEM((here, rows, depth), BF16),
            pltpu.VMEM((here, rows, depth), BF16),
            pltpu.VMEM((here, past, depth), BF16),
            pltpu.VMEM((here, past, depth), BF16),
            pltpu.VMEM((here, reach, rows, depth), BF16),
            pltpu.VMEM((here, reach, rows, depth), BF16),
            dma((2,)),
            dma((4,)),
            dma((here, 4)),
            dma((here, 4, n_head - 1)),
            dma((here, 4, n_head - 1)),
            dma((here, 2, reach)),
            dma((here, 2, reach)),
            dma((here, 2, reach)),
            dma((here, 2, reach)),
            dma((here, 3, n_head - 1)),
            dma((here, 3, n_head - 1)),
        ],
        compiler_params=pltpu.CompilerParams(
            collective_id=0, has_side_effects=True, vmem_limit_bytes=VMEM_ALL
        ),
        cost_estimate=pl.CostEstimate(
            flops=10 * pairs * depth, bytes_accessed=14 * heads * tok * depth, transcendentals=pairs
        ),
    )
    if n_head == 4 and past == rows and heads % 2 == 0 and tok % (2 * depth) == 0:
        call = chain_call(n_ctx, tok, heads, depth, slopes.shape, doc_lengths.shape)
    grads = call(keys_in, values, queries, grad_out, slopes, doc_lengths)
    return pl.pallas_call(
        hand_over,
        out_shape=(out, out, out),
        in_specs=[away] * 3,
        out_specs=(away,) * 3,
        scratch_shapes=[pltpu.VMEM((tok, heads, depth), BF16)] * 3 + [dma((3,)), dma((3,))],
        compiler_params=pltpu.CompilerParams(vmem_limit_bytes=VMEM_ALL),
    )(*grads)


def solution(mesh):
    placed = P(("ctx", "head"), None, None)
    return jax.shard_map(
        body,
        mesh=mesh,
        in_specs=(placed, placed, placed, placed, P(), P()),
        out_specs=(placed, placed, placed),
        check_vma=False,
    )
```

```python
from functools import partial
import math

import jax
import jax.numpy as jnp
from jax import lax
from jax.experimental import pallas as pl
from jax.experimental.pallas import tpu as pltpu
from jax.sharding import PartitionSpec as P

F32 = jnp.float32
BF16 = jnp.bfloat16
VMEM_ALL = 65208320
LOG2E = math.log2(math.e)
NT = (((1,), (1,)), ((), ()))
NN = (((1,), (0,)), ((), ()))
TN = (((0,), (0,)), ((), ()))


def repeat(count, step):
    if count <= 8:
        for n in range(count):
            step(n)
    else:

        def looped(n, carry):
            step(n)
            return carry

        lax.fori_loop(0, count, looped, 0)


def kernel(
    sizes,
    k_hbm, v_hbm, q_hbm, g_hbm, slope_hbm, doc_hbm,
    dq_hbm, dk_hbm, dv_hbm,
    k_raw, v_raw, q_raw, g_raw, k_in, v_in, q_in, g_in, dq_out, dk_out, dv_out, slope_ref, doc_ref, low_ref,
    k_all, v_all, q_all, g_all,
    s_buf, dp_buf, top, low_sum, weighted, dq_acc, dk_acc, dv_acc,
    dq_mine, dk_mine, dv_mine, dk_part, dv_part, dk_got, dv_got,
    small_sem, raw_sem, own_sem, in_send, in_recv, fwd_send, fwd_recv, back_send, back_recv, out_send, out_recv,
):
    n_head, n_ctx, reach, here, tok, rows, depth, tile = sizes
    z = lax.axis_index("head")
    c = lax.axis_index("ctx")
    past = reach * rows
    chunks = (past + tile) // tile
    inv_scale = 1.0 / math.sqrt(depth)

    def peer(off):
        other, bit = z, 1
        while bit < n_head:
            if off & bit:
                other = other + bit * (1 - 2 * lax.rem(z // bit, 2))
            bit *= 2
        return other

    offs = tuple(range(1, n_head))

    def along(off):
        return lax.rem(c + off + n_ctx, n_ctx)

    wholes = (k_hbm, v_hbm, q_hbm, g_hbm)
    raws = (k_raw, v_raw, q_raw, g_raw)

    def raw_copy(a):
        return pltpu.make_async_copy(wholes[a], raws[a], raw_sem.at[a])

    for a in range(4):
        raw_copy(a).start()
    small = (
        pltpu.make_async_copy(slope_hbm, slope_ref, small_sem.at[0]),
        pltpu.make_async_copy(doc_hbm, doc_ref, small_sem.at[1]),
    )
    for copy in small:
        copy.start()

    barrier = pltpu.get_barrier_semaphore()
    for off in range(1, n_head):
        pl.semaphore_signal(barrier, inc=1, device_id={"head": peer(off)}, device_id_type=pl.DeviceIdType.MESH)
    for off in range(1, reach + 1):
        for side in (off, -off):
            pl.semaphore_signal(barrier, inc=1, device_id={"ctx": along(side)}, device_id_type=pl.DeviceIdType.MESH)

    sources = (k_in, v_in, q_in, g_in)
    holders = (k_all, v_all, q_all, g_all)
    bases = (past, past, 0, 0)

    def own_copy(i, a):
        return pltpu.make_async_copy(
            sources[a].at[z * here + i],
            holders[a].at[i, pl.ds(pl.multiple_of(bases[a] + z * tok, tok), tok)],
            own_sem.at[i, a],
        )

    def in_copy(i, a, off):
        return pltpu.make_async_remote_copy(
            src_ref=sources[a].at[peer(off) * here + i],
            dst_ref=holders[a].at[i, pl.ds(pl.multiple_of(bases[a] + z * tok, tok), tok)],
            send_sem=in_send.at[i, a, off - 1],
            recv_sem=in_recv.at[i, a, off - 1],
            device_id={"head": peer(off)},
            device_id_type=pl.DeviceIdType.MESH,
        )

    def fwd_copy(i, a, r):
        return pltpu.make_async_remote_copy(
            src_ref=holders[a].at[i, pl.ds(past, rows)],
            dst_ref=holders[a].at[i, pl.ds((reach - r) * rows, rows)],
            send_sem=fwd_send.at[i, a, r - 1],
            recv_sem=fwd_recv.at[i, a, r - 1],
            device_id={"ctx": along(r)},
            device_id_type=pl.DeviceIdType.MESH,
        )

    parts = (dk_part, dv_part)
    gots = (dk_got, dv_got)

    def back_copy(i, a, r):
        return pltpu.make_async_remote_copy(
            src_ref=parts[a].at[i, pl.ds((reach - r) * rows, rows)],
            dst_ref=gots[a].at[i, r - 1],
            send_sem=back_send.at[i, a, r - 1],
            recv_sem=back_recv.at[i, a, r - 1],
            device_id={"ctx": along(-r)},
            device_id_type=pl.DeviceIdType.MESH,
        )

    mine = (dq_mine, dk_mine, dv_mine)
    outs = (dq_out, dk_out, dv_out)

    def out_copy(i, a, off):
        return pltpu.make_async_remote_copy(
            src_ref=mine[a].at[i, pl.ds(pl.multiple_of(peer(off) * tok, tok), tok)],
            dst_ref=outs[a].at[z * here + i],
            send_sem=out_send.at[i, a, off - 1],
            recv_sem=out_recv.at[i, a, off - 1],
            device_id={"head": peer(off)},
            device_id_type=pl.DeviceIdType.MESH,
        )

    def send_out(i, a):
        for off in offs:
            out_copy(i, a, off).start()
        outs[a][z * here + i] = mine[a][i, pl.ds(pl.multiple_of(z * tok, tok), tok)]

    def arrived(i, a):
        own_copy(i, a).wait()
        for off in range(1, n_head):
            in_copy(i, a, off).wait_recv()

    def attend(i):
        slope2 = slope_ref[z * here + i] * LOG2E
        dk_acc[...] = jnp.zeros_like(dk_acc)
        dv_acc[...] = jnp.zeros_like(dv_acc)

        def block(b, carry):
            first = pl.multiple_of(b * tile, tile)
            q = q_all[i, pl.ds(first, tile)]
            g = g_all[i, pl.ds(first, tile)]
            low = low_ref[:, pl.ds(first, tile)] + (past - first).astype(F32)
            high = past + lax.broadcasted_iota(jnp.int32, (1, tile), 1)
            high = high.astype(F32)
            spot = lax.broadcasted_iota(jnp.int32, (tile, tile), 0).astype(F32)
            top[...] = jnp.full_like(top, -1e30)
            low_sum[...] = jnp.zeros_like(low_sum)
            weighted[...] = jnp.zeros_like(weighted)
            dq_acc[...] = jnp.zeros_like(dq_acc)

            def window(n):
                return pl.ds(pl.multiple_of(first + n * tile, tile), tile)

            def held(n):
                return pl.ds(pl.multiple_of(n * tile, tile), tile)

            def score(n):
                raw = lax.dot_general(k_all[i, window(n)], q, NT, preferred_element_type=F32)
                where = spot + jnp.float32(n * tile)
                s = raw * (inv_scale * LOG2E) + slope2 * (where - past)
                s = jnp.where((where >= low) & (where <= high), s, -1e30)
                s_buf[held(n)] = s
                top[...] = jnp.maximum(top[...], jnp.max(s, axis=0, keepdims=True))

            def weigh(n):
                p = jnp.exp2(s_buf[held(n)] - top[...])
                dp = lax.dot_general(v_all[i, window(n)], g, NT, preferred_element_type=F32)
                s_buf[held(n)] = p
                dp_buf[held(n)] = dp
                low_sum[...] += jnp.sum(p, axis=0, keepdims=True)
                weighted[...] += jnp.sum(p * dp, axis=0, keepdims=True)

            repeat(chunks, score)
            repeat(chunks, weigh)
            share = 1.0 / low_sum[...]
            delta = weighted[...] * share

            def spread(n):
                w = s_buf[held(n)] * share
                ds = (w * (dp_buf[held(n)] - delta)).astype(BF16)
                dv_acc[window(n)] += lax.dot_general(w.astype(BF16), g, NN, preferred_element_type=F32)
                dk_acc[window(n)] += lax.dot_general(ds, q, NN, preferred_element_type=F32)
                dq_acc[...] += lax.dot_general(k_all[i, window(n)], ds, TN, preferred_element_type=F32)

            repeat(chunks, spread)
            dq_mine[i, pl.ds(first, tile)] = (dq_acc[...] * inv_scale).T.astype(BF16)
            return carry

        lax.fori_loop(0, rows // tile, block, 0)
        dk_part[i] = dk_acc[pl.ds(0, past)].astype(BF16)
        dv_part[i] = dv_acc[pl.ds(0, past)].astype(BF16)

    def settle(i, a, acc, scale):
        total = acc
        for r in range(1, reach + 1):
            back_copy(i, a, r).wait_recv()
            total = total + gots[a][i, r - 1].astype(F32)
        mine[1 + a][i] = (total * scale).astype(BF16)
        send_out(i, 1 + a)

    def start_head(i, a):
        for off in offs:
            in_copy(i, a, off).start()
        own_copy(i, a).start()

    def turn(source, target, count):
        if source.shape[0] == tok:
            for n in range(0, tok, count):
                target[:, n : n + count] = jnp.swapaxes(source[n : n + count], 0, 1)
        else:
            for n in range(0, tok, count):
                target[n : n + count] = jnp.swapaxes(source[:, n : n + count], 0, 1)

    step = min(64, tok)
    for a in range(4):
        raw_copy(a).wait()
        turn(raws[a], sources[a], step)
        if a == 0:
            pl.semaphore_wait(barrier, n_head - 1 + 2 * reach)
        start_head(0, a)
    for i in range(1, here):
        for a in range(4):
            start_head(i, a)

    for copy in small:
        copy.wait()
    spots = lax.broadcasted_iota(jnp.int32, (1, rows), 1) + c * rows
    start = jnp.int32(0)
    low = jnp.zeros((1, rows), jnp.int32)
    for n in range(doc_ref.shape[0]):
        low = jnp.where(spots >= start, start, low)
        start = start + doc_ref[n]
    low_ref[...] = (low - c * rows).astype(F32)

    def forward(i):
        for a in range(2):
            arrived(i, a)
            for r in range(1, reach + 1):
                fwd_copy(i, a, r).start()

    forward(0)
    for i in range(here):
        for a in (2, 3):
            arrived(i, a)
        for a in range(2):
            for r in range(1, reach + 1):
                fwd_copy(i, a, r).wait_recv()
        attend(i)
        for a in range(2):
            for r in range(1, reach + 1):
                back_copy(i, a, r).start()
        send_out(i, 0)
        if i + 1 < here:
            forward(i + 1)
        settle(i, 0, dk_acc[pl.ds(past, rows)], inv_scale)
        settle(i, 1, dv_acc[pl.ds(past, rows)], 1.0)

    results = (dq_hbm, dk_hbm, dv_hbm)

    def result_copy(a):
        return pltpu.make_async_copy(raws[a], results[a], raw_sem.at[a])

    for a in range(3):
        for i in range(here):
            for off in offs:
                out_copy(i, a, off).wait_recv()
        turn(outs[a], raws[a], step)
        result_copy(a).start()

    for i in range(here):
        for off in offs:
            for a in range(4):
                in_copy(i, a, off).wait_send()
            for a in range(3):
                out_copy(i, a, off).wait_send()
        for a in range(2):
            for r in range(1, reach + 1):
                fwd_copy(i, a, r).wait_send()
                back_copy(i, a, r).wait_send()
    for a in range(3):
        result_copy(a).wait()


def chain_kernel(
    sizes,
    k_hbm, v_hbm, q_hbm, g_hbm, slope_hbm, doc_hbm,
    dq_hbm, dk_hbm, dv_hbm,
    k_raw, v_raw, q_raw, g_raw, k_in, v_in, q_in, g_in, dq_out, dk_out, dv_out, slope_ref, doc_ref, low_ref,
    k_all, v_all, q_all, g_all,
    p_buf, dp_buf, top, stat, stat_got, both, dq_acc, dk_acc, dv_acc, dq_rows,
    dq_own, dq_next, dq_far, got_next, got_far, got_side, dq_pair, dk_pair, dv_pair, got_pair,
    small_sem, raw_sem, own_sem, in_send, in_recv, near_send, near_recv, far_send, far_recv,
    stat_send, stat_recv, next_send, next_recv, side_recv, back_send, back_recv, pair_send, pair_recv,
):
    n_ctx, mine, tok, depth = sizes
    z = lax.axis_index("head")
    c = lax.axis_index("ctx")
    side = z // 2
    half = lax.rem(z, 2)
    rest = 1 - half
    chunk = 2 * tok
    span = 3 * chunk
    first_key = (2 * c + side) * chunk
    inner = lax.rem(side + half, 2) == 1
    outer = lax.rem(side + half, 2) == 0
    inv_scale = 1.0 / math.sqrt(depth)

    before, after = lax.rem(c - 1 + n_ctx, n_ctx), lax.rem(c + 1, n_ctx)
    c_less = lax.rem(c - (1 - side) + n_ctx, n_ctx)
    c_more = lax.rem(c + side, n_ctx)
    across = z + 2 - 4 * side
    mirror = 3 - z
    twin = {"head": z + 1 - 2 * half}
    less_one, more_one = {"ctx": c_less, "head": across}, {"ctx": c_more, "head": across}
    less_mirror, more_mirror = {"ctx": c_less, "head": mirror}, {"ctx": c_more, "head": mirror}
    less_two, more_two = {"ctx": before}, {"ctx": after}

    def remote(src, dst, send, recv, device):
        return pltpu.make_async_remote_copy(
            src_ref=src, dst_ref=dst, send_sem=send, recv_sem=recv,
            device_id=device, device_id_type=pl.DeviceIdType.MESH,
        )

    wholes = (k_hbm, v_hbm, q_hbm, g_hbm)
    raws = (k_raw, v_raw, q_raw, g_raw)
    sources = (k_in, v_in, q_in, g_in)
    holders = (k_all, v_all, q_all, g_all)

    def raw_copy(a):
        return pltpu.make_async_copy(wholes[a], raws[a], raw_sem.at[a])

    for a in (2, 3, 0, 1):
        raw_copy(a).start()
    small = (
        pltpu.make_async_copy(slope_hbm, slope_ref, small_sem.at[0]),
        pltpu.make_async_copy(doc_hbm, doc_ref, small_sem.at[1]),
    )
    for copy in small:
        copy.start()

    barrier = pltpu.get_barrier_semaphore()

    def greet(device):
        pl.semaphore_signal(barrier, inc=1, device_id=device, device_id_type=pl.DeviceIdType.MESH)

    greet(more_one)
    greet(more_two)
    greet(twin)

    @pl.when(inner)
    def _():
        greet(more_mirror)

    def block(base, which):
        return pl.ds(pl.multiple_of(base + which * tok, tok), tok)

    def own_copy(i, a):
        return pltpu.make_async_copy(sources[a].at[half * mine + i], holders[a].at[i, block(0, half)], own_sem.at[i, a])

    def in_copy(i, a):
        return remote(
            sources[a].at[rest * mine + i], holders[a].at[i, block(0, half)], in_send.at[i, a], in_recv.at[i, a], twin
        )

    def near_own(i, a):
        return remote(
            sources[a].at[half * mine + i], holders[a].at[i, block(chunk, half)],
            near_send.at[i, a - 2, 0], near_recv.at[i, a - 2, half], less_one,
        )

    def near_other(i, a):
        return remote(
            sources[a].at[rest * mine + i], holders[a].at[i, block(chunk, half)],
            near_send.at[i, a - 2, 1], near_recv.at[i, a - 2, half], less_mirror,
        )

    def near_relay(i, a):
        return remote(
            holders[a].at[i, block(0, rest)], holders[a].at[i, block(chunk, rest)],
            near_send.at[i, a - 2, 2], near_recv.at[i, a - 2, rest], less_one,
        )

    def far_copy(i, a):
        return remote(
            holders[a].at[i, pl.ds(0, chunk)], holders[a].at[i, pl.ds(2 * chunk, chunk)],
            far_send.at[i, a - 2], far_recv.at[i, a - 2], less_two,
        )

    routes = (
        (0, less_one, 1, 0),
        (0, less_two, 2, 0),
        (1, more_one, 0, 0),
        (1, less_one, 2, 1),
        (2, more_two, 0, 1),
        (2, more_one, 1, 1),
    )

    def stat_copy(i, m):
        slot, device, there, place = routes[m]
        return remote(
            stat.at[i, slot], stat_got.at[i, there, place], stat_send.at[i, m], stat_recv.at[i, there, place], device
        )

    def next_own(i):
        return remote(
            dq_next.at[i, block(0, half)], got_next.at[i], next_send.at[i, 0], next_recv.at[i], more_one
        )

    def next_side(i):
        kind = lax.rem(side + half + 1, 2)
        device = {"ctx": c_more, "head": 2 - side}
        return remote(
            dq_next.at[i, block(0, rest)], got_side.at[kind, i], next_send.at[i, 1], side_recv.at[kind, i], device
        )

    def back_copy(i):
        return remote(dq_far.at[i], got_far.at[i], back_send.at[i], back_recv.at[i], more_two)

    pairs = (dq_pair, dk_pair, dv_pair)
    pair_targets = (None, dk_out, dv_out)

    def pair_copy(i, a):
        target = got_pair.at[i] if a == 0 else pair_targets[a].at[half * mine + i]
        return remote(pairs[a].at[i], target, pair_send.at[i, a], pair_recv.at[i, a], twin)

    def pair_wait(i, a):
        target = got_pair.at[i] if a == 0 else pair_targets[a].at[rest * mine + i]
        remote(pairs[a].at[i], target, pair_send.at[i, a], pair_recv.at[i, a], twin).wait_recv()

    step = min(64, tok)

    def turn(source, target):
        if source.shape[0] == tok:
            for n in range(0, tok, step):
                target[:, n : n + step] = jnp.swapaxes(source[n : n + step], 0, 1)
        else:
            for n in range(0, tok, step):
                target[n : n + step] = jnp.swapaxes(source[:, n : n + step], 0, 1)

    def open_head(i, a):
        in_copy(i, a).start()
        own_copy(i, a).start()
        if a >= 2:
            near_own(i, a).start()

            @pl.when(inner)
            def _():
                near_other(i, a).start()

    def relay(i):
        for a in (2, 3):
            own_copy(i, a).wait()
            in_copy(i, a).wait_recv()
            far_copy(i, a).start()

            @pl.when(inner)
            def _():
                near_relay(i, a).start()

    def arrived(i):
        for a in (0, 1):
            own_copy(i, a).wait()
            in_copy(i, a).wait_recv()
        for a in (2, 3):
            far_copy(i, a).wait_recv()
            near_own(i, a).wait_recv()
            near_relay(i, a).wait_recv()

    def tile_rows(t):
        return pl.ds(pl.multiple_of(t * tok, tok), tok)

    def gather(i, slot_of):
        slope2 = slope_ref[half * mine + i] * LOG2E

        def slot_step(slot, carry):
            for u in range(2):
                t = 2 * slot + u
                q = q_all[i, tile_rows(t)]
                g = g_all[i, tile_rows(t)]
                low = low_ref[:, tile_rows(t)]
                first = (t * tok).astype(F32)
                high = lax.broadcasted_iota(jnp.int32, (1, tok), 1).astype(F32) + first
                spot = lax.broadcasted_iota(jnp.int32, (tok, tok), 0).astype(F32)
                best = jnp.full((1, tok), -1e30, F32)
                for b in range(2):
                    raw = lax.dot_general(k_all[i, b * tok : (b + 1) * tok], q, NT, preferred_element_type=F32)
                    where = spot + jnp.float32(b * tok)
                    s = raw * (inv_scale * LOG2E) + slope2 * (where - first)
                    s = jnp.where((where >= low) & (where <= high), s, -1e30)
                    p_buf[slot_of, t, b] = s
                    best = jnp.maximum(best, jnp.max(s, axis=0, keepdims=True))
                total = jnp.zeros((1, tok), F32)
                weighted = jnp.zeros((1, tok), F32)
                for b in range(2):
                    p = jnp.exp2(p_buf[slot_of, t, b] - best)
                    dp = lax.dot_general(v_all[i, b * tok : (b + 1) * tok], g, NT, preferred_element_type=F32)
                    p_buf[slot_of, t, b] = p
                    dp_buf[slot_of, t, b] = dp
                    total = total + jnp.sum(p, axis=0, keepdims=True)
                    weighted = weighted + jnp.sum(p * dp, axis=0, keepdims=True)
                top[slot_of, t] = best
                level = best + jnp.log2(total)
                share = weighted / total
                for r in range(lanes):
                    row = u * lanes + r
                    part = slice(r * depth, (r + 1) * depth)
                    stat[i, slot, row : row + 1] = level[:, part]
                    stat[i, slot, 2 * lanes + row : 2 * lanes + row + 1] = share[:, part]
            return carry

        lax.fori_loop(0, 3, slot_step, 0)
        for m in range(6):
            stat_copy(i, m).start()

    lanes = tok // depth

    def spread(i, slot_of):
        for slot in range(3):
            for place in range(2):
                remote(
                    stat.at[i, slot], stat_got.at[i, slot, place], stat_send.at[i, 0], stat_recv.at[i, slot, place], twin
                ).wait_recv()
            found = (stat[i, slot], stat_got[i, slot, 0], stat_got[i, slot, 1])
            levels = [x[: 2 * lanes] for x in found]
            shares = [x[2 * lanes :] for x in found]
            peak = jnp.maximum(jnp.maximum(levels[0], levels[1]), levels[2])
            full = peak + jnp.log2(sum(jnp.exp2(x - peak) for x in levels))
            delta = sum(jnp.exp2(x - full) * y for x, y in zip(levels, shares))
            for u in range(2):
                for r in range(lanes):
                    row = u * lanes + r
                    part = slice(r * depth, (r + 1) * depth)
                    both[0, 2 * slot + u, :, part] = full[row : row + 1]
                    both[1, 2 * slot + u, :, part] = delta[row : row + 1]
        dk_acc[...] = jnp.zeros_like(dk_acc)
        dv_acc[...] = jnp.zeros_like(dv_acc)

        def tile_step(t, carry):
            q = q_all[i, tile_rows(t)]
            g = g_all[i, tile_rows(t)]
            share = jnp.exp2(top[slot_of, t] - both[0, t])
            delta = both[1, t]
            for b in range(2):
                rows = slice(b * tok, (b + 1) * tok)
                w = p_buf[slot_of, t, b] * share
                ds = (w * (dp_buf[slot_of, t, b] - delta)).astype(BF16)
                dv_acc[rows] += lax.dot_general(w.astype(BF16), g, NN, preferred_element_type=F32)
                dk_acc[rows] += lax.dot_general(ds, q, NN, preferred_element_type=F32)
                part = lax.dot_general(k_all[i, rows], ds, TN, preferred_element_type=F32)
                if b == 0:
                    dq_acc[...] = part
                else:
                    dq_acc[...] += part
            dq_rows[tile_rows(t)] = (dq_acc[...] * inv_scale).T
            return carry

        lax.fori_loop(0, 6, tile_step, 0)
        dq_next[i] = dq_rows[chunk : 2 * chunk].astype(BF16)
        dq_far[i] = dq_rows[2 * chunk : 3 * chunk].astype(BF16)
        back_copy(i).start()
        dq_own[i] = dq_rows[0:chunk]
        dk_pair[i] = (dk_acc[block(0, rest)] * inv_scale).astype(BF16)
        pair_copy(i, 1).start()
        dv_pair[i] = dv_acc[block(0, rest)].astype(BF16)
        pair_copy(i, 2).start()
        dk_out[half * mine + i] = (dk_acc[block(0, half)] * inv_scale).astype(BF16)
        dv_out[half * mine + i] = dv_acc[block(0, half)].astype(BF16)

    def send_next(i):
        next_side(i).start()
        next_own(i).start()

    def settle(i):
        back_copy(i).wait_recv()

        @pl.when(inner)
        def _():
            remote(dq_pair.at[i], got_side.at[1, i], next_send.at[i, 1], side_recv.at[1, i], twin).wait_recv()

        dq_pair[i] = (
            dq_own[i, block(0, rest)] + got_far[i, block(0, rest)].astype(F32) + got_side[1, i].astype(F32)
        ).astype(BF16)
        pair_copy(i, 0).start()
        next_own(i).wait_recv()
        dq_out[half * mine + i] = (
            dq_own[i, block(0, half)] + got_far[i, block(0, half)].astype(F32) + got_next[i].astype(F32)
        ).astype(BF16)

    def close(i):
        pair_wait(i, 0)

        @pl.when(inner)
        def _():
            remote(dq_pair.at[i], got_side.at[0, i], next_send.at[i, 1], side_recv.at[0, i], twin).wait_recv()

        dq_out[rest * mine + i] = (got_pair[i].astype(F32) + got_side[0, i].astype(F32)).astype(BF16)

    for a in (2, 3, 0, 1):
        raw_copy(a).wait()
        turn(raws[a], sources[a])
        if a == 2:
            pl.semaphore_wait(barrier, 3 + lax.rem(side + half, 2))
        open_head(0, a)
    for a in (2, 3, 0, 1):
        if mine > 1:
            open_head(1, a)

    @pl.when(outer)
    def _():
        got_side[...] = jnp.zeros_like(got_side)

    for copy in small:
        copy.wait()
    spots = lax.broadcasted_iota(jnp.int32, (1, span), 1) + first_key
    start = jnp.int32(0)
    low = jnp.zeros((1, span), jnp.int32)
    for n in range(doc_ref.shape[0]):
        low = jnp.where(spots >= start, start, low)
        start = start + doc_ref[n]
    low = jnp.where(spots >= start, spots + 1, low)
    low_ref[...] = (low - first_key).astype(F32)

    relay(0)
    if mine > 1:
        relay(1)
    held = []
    for i in range(mine):
        if i + 2 < mine:
            for a in (2, 3, 0, 1):
                open_head(i + 2, a)
        arrived(i)
        gather(i, i % 2)
        for m in held:
            send_next(m)
        held = []
        if i >= 1:
            spread(i - 1, (i - 1) % 2)
            held = [i - 1]
        if i + 2 < mine:
            relay(i + 2)
        if i + 3 >= mine and i + 1 < mine and i + 2 < mine:
            for m in held:
                send_next(m)
            held = []
    for m in held:
        send_next(m)
    spread(mine - 1, (mine - 1) % 2)
    send_next(mine - 1)
    for i in range(mine):
        settle(i)

    results = (dq_hbm, dk_hbm, dv_hbm)
    outs = (dq_out, dk_out, dv_out)

    def result_copy(a):
        return pltpu.make_async_copy(raws[a], results[a], raw_sem.at[a])

    for a in (1, 2):
        for i in range(mine):
            pair_wait(i, a)
        turn(outs[a], raws[a])
        result_copy(a).start()
    for i in range(mine):
        close(i)
    turn(outs[0], raws[0])
    result_copy(0).start()

    for i in range(mine):
        for a in range(4):
            in_copy(i, a).wait_send()
        for a in (2, 3):
            near_own(i, a).wait_send()
            far_copy(i, a).wait_send()
        for m in range(6):
            stat_copy(i, m).wait_send()
        next_own(i).wait_send()
        next_side(i).wait_send()
        back_copy(i).wait_send()
        for a in range(3):
            pair_copy(i, a).wait_send()

    @pl.when(inner)
    def _():
        for i in range(mine):
            for a in (2, 3):
                near_other(i, a).wait_send()
                near_relay(i, a).wait_send()

    for a in range(3):
        result_copy(a).wait()


def chain_call(n_ctx, tok, heads, depth, slots, docs):
    mine = heads // 2
    chunk = 2 * tok
    away = pl.BlockSpec(memory_space=pl.ANY)
    dma = pltpu.SemaphoreType.DMA
    out = jax.ShapeDtypeStruct((tok, heads, depth), BF16)
    pairs = mine * 6 * chunk * tok
    return pl.pallas_call(
        partial(chain_kernel, (n_ctx, mine, tok, depth)),
        out_shape=(out, out, out),
        in_specs=[away] * 6,
        out_specs=(away,) * 3,
        scratch_shapes=[pltpu.VMEM((tok, heads, depth), BF16)] * 4
        + [pltpu.VMEM((heads, tok, depth), BF16)] * 7
        + [
            pltpu.SMEM(slots, F32),
            pltpu.SMEM(docs, jnp.int32),
            pltpu.VMEM((1, 3 * chunk), F32),
            pltpu.VMEM((mine, chunk, depth), BF16),
            pltpu.VMEM((mine, chunk, depth), BF16),
            pltpu.VMEM((mine, 3 * chunk, depth), BF16),
            pltpu.VMEM((mine, 3 * chunk, depth), BF16),
            pltpu.VMEM((2, 6, 2, tok, tok), F32),
            pltpu.VMEM((2, 6, 2, tok, tok), F32),
            pltpu.VMEM((2, 6, 1, tok), F32),
            pltpu.VMEM((mine, 3, 4 * tok // depth, depth), F32),
            pltpu.VMEM((mine, 3, 2, 4 * tok // depth, depth), F32),
            pltpu.VMEM((2, 6, 1, tok), F32),
            pltpu.VMEM((depth, tok), F32),
            pltpu.VMEM((chunk, depth), F32),
            pltpu.VMEM((chunk, depth), F32),
            pltpu.VMEM((3 * chunk, depth), F32),
            pltpu.VMEM((mine, chunk, depth), F32),
            pltpu.VMEM((mine, chunk, depth), BF16),
            pltpu.VMEM((mine, chunk, depth), BF16),
            pltpu.VMEM((mine, tok, depth), BF16),
            pltpu.VMEM((mine, chunk, depth), BF16),
            pltpu.VMEM((2, mine, tok, depth), BF16),
            pltpu.VMEM((mine, tok, depth), BF16),
            pltpu.VMEM((mine, tok, depth), BF16),
            pltpu.VMEM((mine, tok, depth), BF16),
            pltpu.VMEM((mine, tok, depth), BF16),
            dma((2,)),
            dma((4,)),
            dma((mine, 4)),
            dma((mine, 4)),
            dma((mine, 4)),
            dma((mine, 2, 3)),
            dma((mine, 2, 2)),
            dma((mine, 2)),
            dma((mine, 2)),
            dma((mine, 6)),
            dma((mine, 3, 2)),
            dma((mine, 2)),
            dma((mine,)),
            dma((2, mine)),
            dma((mine,)),
            dma((mine,)),
            dma((mine, 3)),
            dma((mine, 3)),
        ],
        compiler_params=pltpu.CompilerParams(
            collective_id=1, has_side_effects=True, vmem_limit_bytes=VMEM_ALL
        ),
        cost_estimate=pl.CostEstimate(
            flops=10 * pairs * depth, bytes_accessed=14 * heads * tok * depth, transcendentals=pairs
        ),
    )


def hand_over(a_in, b_in, c_in, a_out, b_out, c_out, a_buf, b_buf, c_buf, in_sem, out_sem):
    bufs = (a_buf, b_buf, c_buf)
    ins = [pltpu.make_async_copy(x, bufs[n], in_sem.at[n]) for n, x in enumerate((a_in, b_in, c_in))]
    outs = [pltpu.make_async_copy(bufs[n], x, out_sem.at[n]) for n, x in enumerate((a_out, b_out, c_out))]
    for copy in ins:
        copy.start()
    for arrive, leave in zip(ins, outs):
        arrive.wait()
        leave.start()
    for copy in outs:
        copy.wait()


def body(queries, keys_in, values, grad_out, slopes, doc_lengths):
    n_head = lax.axis_size("head")
    n_ctx = lax.axis_size("ctx")
    tok, heads, depth = queries.shape
    here = heads // n_head
    rows = tok * n_head
    span = min(16384, rows * n_ctx // 8)
    reach = span // rows
    past = reach * rows
    tile = min(256, rows)
    sizes = (n_head, n_ctx, reach, here, tok, rows, depth, tile)
    away = pl.BlockSpec(memory_space=pl.ANY)
    dma = pltpu.SemaphoreType.DMA
    out = jax.ShapeDtypeStruct((tok, heads, depth), BF16)
    swapped = pltpu.VMEM((heads, tok, depth), BF16)
    window = past + tile
    pairs = rows * window * here
    call = pl.pallas_call(
        partial(kernel, sizes),
        out_shape=(out, out, out),
        in_specs=[away] * 6,
        out_specs=(away,) * 3,
        scratch_shapes=[pltpu.VMEM((tok, heads, depth), BF16)] * 4
        + [swapped] * 7
        + [
            pltpu.SMEM(slopes.shape, F32),
            pltpu.SMEM(doc_lengths.shape, jnp.int32),
            pltpu.VMEM((1, rows), F32),
            pltpu.VMEM((here, past + rows, depth), BF16),
            pltpu.VMEM((here, past + rows, depth), BF16),
            pltpu.VMEM((here, rows, depth), BF16),
            pltpu.VMEM((here, rows, depth), BF16),
            pltpu.VMEM((window, tile), F32),
            pltpu.VMEM((window, tile), F32),
            pltpu.VMEM((1, tile), F32),
            pltpu.VMEM((1, tile), F32),
            pltpu.VMEM((1, tile), F32),
            pltpu.VMEM((depth, tile), F32),
            pltpu.VMEM((past + rows, depth), F32),
            pltpu.VMEM((past + rows, depth), F32),
            pltpu.VMEM((here, rows, depth), BF16),
            pltpu.VMEM((here, rows, depth), BF16),
            pltpu.VMEM((here, rows, depth), BF16),
            pltpu.VMEM((here, past, depth), BF16),
            pltpu.VMEM((here, past, depth), BF16),
            pltpu.VMEM((here, reach, rows, depth), BF16),
            pltpu.VMEM((here, reach, rows, depth), BF16),
            dma((2,)),
            dma((4,)),
            dma((here, 4)),
            dma((here, 4, n_head - 1)),
            dma((here, 4, n_head - 1)),
            dma((here, 2, reach)),
            dma((here, 2, reach)),
            dma((here, 2, reach)),
            dma((here, 2, reach)),
            dma((here, 3, n_head - 1)),
            dma((here, 3, n_head - 1)),
        ],
        compiler_params=pltpu.CompilerParams(
            collective_id=0, has_side_effects=True, vmem_limit_bytes=VMEM_ALL
        ),
        cost_estimate=pl.CostEstimate(
            flops=10 * pairs * depth, bytes_accessed=14 * heads * tok * depth, transcendentals=pairs
        ),
    )
    if n_head == 4 and past == rows and heads % 2 == 0 and tok % (2 * depth) == 0:
        call = chain_call(n_ctx, tok, heads, depth, slopes.shape, doc_lengths.shape)
    grads = call(keys_in, values, queries, grad_out, slopes, doc_lengths)
    return pl.pallas_call(
        hand_over,
        out_shape=(out, out, out),
        in_specs=[away] * 3,
        out_specs=(away,) * 3,
        scratch_shapes=[pltpu.VMEM((tok, heads, depth), BF16)] * 3 + [dma((3,)), dma((3,))],
        compiler_params=pltpu.CompilerParams(vmem_limit_bytes=VMEM_ALL),
    )(*grads)


def solution(mesh):
    placed = P(("ctx", "head"), None, None)
    return jax.shard_map(
        body,
        mesh=mesh,
        in_specs=(placed, placed, placed, placed, P(), P()),
        out_specs=(placed, placed, placed),
        check_vma=False,
    )
```

```python
from functools import partial
import math

import jax
import jax.numpy as jnp
from jax import lax
from jax.experimental import pallas as pl
from jax.experimental.pallas import tpu as pltpu
from jax.sharding import PartitionSpec as P

F32 = jnp.float32
BF16 = jnp.bfloat16
VMEM_ALL = 65208320
VMEM_PART = 48 << 20
LOG2E = math.log2(math.e)
NT = (((1,), (1,)), ((), ()))
NN = (((1,), (0,)), ((), ()))
TN = (((0,), (0,)), ((), ()))


def repeat(count, step):
    if count <= 8:
        for n in range(count):
            step(n)
    else:

        def looped(n, carry):
            step(n)
            return carry

        lax.fori_loop(0, count, looped, 0)


def kernel(
    sizes,
    k_hbm, v_hbm, q_hbm, g_hbm, slope_hbm, doc_hbm,
    dq_hbm, dk_hbm, dv_hbm,
    k_raw, v_raw, q_raw, g_raw, k_in, v_in, q_in, g_in, dq_out, dk_out, dv_out, slope_ref, doc_ref, low_ref,
    k_all, v_all, q_all, g_all,
    s_buf, dp_buf, top, low_sum, weighted, dq_acc, dk_acc, dv_acc,
    dq_mine, dk_mine, dv_mine, dk_part, dv_part, dk_got, dv_got,
    small_sem, raw_sem, own_sem, in_send, in_recv, fwd_send, fwd_recv, back_send, back_recv, out_send, out_recv,
):
    n_head, n_ctx, reach, here, tok, rows, depth, tile = sizes
    z = lax.axis_index("head")
    c = lax.axis_index("ctx")
    past = reach * rows
    chunks = (past + tile) // tile
    inv_scale = 1.0 / math.sqrt(depth)

    def peer(off):
        other, bit = z, 1
        while bit < n_head:
            if off & bit:
                other = other + bit * (1 - 2 * lax.rem(z // bit, 2))
            bit *= 2
        return other

    offs = tuple(range(1, n_head))

    def along(off):
        return lax.rem(c + off + n_ctx, n_ctx)

    wholes = (k_hbm, v_hbm, q_hbm, g_hbm)
    raws = (k_raw, v_raw, q_raw, g_raw)

    def raw_copy(a):
        return pltpu.make_async_copy(wholes[a], raws[a], raw_sem.at[a])

    for a in range(4):
        raw_copy(a).start()
    small = (
        pltpu.make_async_copy(slope_hbm, slope_ref, small_sem.at[0]),
        pltpu.make_async_copy(doc_hbm, doc_ref, small_sem.at[1]),
    )
    for copy in small:
        copy.start()

    barrier = pltpu.get_barrier_semaphore()
    for off in range(1, n_head):
        pl.semaphore_signal(barrier, inc=1, device_id={"head": peer(off)}, device_id_type=pl.DeviceIdType.MESH)
    for off in range(1, reach + 1):
        for side in (off, -off):
            pl.semaphore_signal(barrier, inc=1, device_id={"ctx": along(side)}, device_id_type=pl.DeviceIdType.MESH)

    sources = (k_in, v_in, q_in, g_in)
    holders = (k_all, v_all, q_all, g_all)
    bases = (past, past, 0, 0)

    def own_copy(i, a):
        return pltpu.make_async_copy(
            sources[a].at[z * here + i],
            holders[a].at[i, pl.ds(pl.multiple_of(bases[a] + z * tok, tok), tok)],
            own_sem.at[i, a],
        )

    def in_copy(i, a, off):
        return pltpu.make_async_remote_copy(
            src_ref=sources[a].at[peer(off) * here + i],
            dst_ref=holders[a].at[i, pl.ds(pl.multiple_of(bases[a] + z * tok, tok), tok)],
            send_sem=in_send.at[i, a, off - 1],
            recv_sem=in_recv.at[i, a, off - 1],
            device_id={"head": peer(off)},
            device_id_type=pl.DeviceIdType.MESH,
        )

    def fwd_copy(i, a, r):
        return pltpu.make_async_remote_copy(
            src_ref=holders[a].at[i, pl.ds(past, rows)],
            dst_ref=holders[a].at[i, pl.ds((reach - r) * rows, rows)],
            send_sem=fwd_send.at[i, a, r - 1],
            recv_sem=fwd_recv.at[i, a, r - 1],
            device_id={"ctx": along(r)},
            device_id_type=pl.DeviceIdType.MESH,
        )

    parts = (dk_part, dv_part)
    gots = (dk_got, dv_got)

    def back_copy(i, a, r):
        return pltpu.make_async_remote_copy(
            src_ref=parts[a].at[i, pl.ds((reach - r) * rows, rows)],
            dst_ref=gots[a].at[i, r - 1],
            send_sem=back_send.at[i, a, r - 1],
            recv_sem=back_recv.at[i, a, r - 1],
            device_id={"ctx": along(-r)},
            device_id_type=pl.DeviceIdType.MESH,
        )

    mine = (dq_mine, dk_mine, dv_mine)
    outs = (dq_out, dk_out, dv_out)

    def out_copy(i, a, off):
        return pltpu.make_async_remote_copy(
            src_ref=mine[a].at[i, pl.ds(pl.multiple_of(peer(off) * tok, tok), tok)],
            dst_ref=outs[a].at[z * here + i],
            send_sem=out_send.at[i, a, off - 1],
            recv_sem=out_recv.at[i, a, off - 1],
            device_id={"head": peer(off)},
            device_id_type=pl.DeviceIdType.MESH,
        )

    def send_out(i, a):
        for off in offs:
            out_copy(i, a, off).start()
        outs[a][z * here + i] = mine[a][i, pl.ds(pl.multiple_of(z * tok, tok), tok)]

    def arrived(i, a):
        own_copy(i, a).wait()
        for off in range(1, n_head):
            in_copy(i, a, off).wait_recv()

    def attend(i):
        slope2 = slope_ref[z * here + i] * LOG2E
        dk_acc[...] = jnp.zeros_like(dk_acc)
        dv_acc[...] = jnp.zeros_like(dv_acc)

        def block(b, carry):
            first = pl.multiple_of(b * tile, tile)
            q = q_all[i, pl.ds(first, tile)]
            g = g_all[i, pl.ds(first, tile)]
            low = low_ref[:, pl.ds(first, tile)] + (past - first).astype(F32)
            high = past + lax.broadcasted_iota(jnp.int32, (1, tile), 1)
            high = high.astype(F32)
            spot = lax.broadcasted_iota(jnp.int32, (tile, tile), 0).astype(F32)
            top[...] = jnp.full_like(top, -1e30)
            low_sum[...] = jnp.zeros_like(low_sum)
            weighted[...] = jnp.zeros_like(weighted)
            dq_acc[...] = jnp.zeros_like(dq_acc)

            def window(n):
                return pl.ds(pl.multiple_of(first + n * tile, tile), tile)

            def held(n):
                return pl.ds(pl.multiple_of(n * tile, tile), tile)

            def score(n):
                raw = lax.dot_general(k_all[i, window(n)], q, NT, preferred_element_type=F32)
                where = spot + jnp.float32(n * tile)
                s = raw * (inv_scale * LOG2E) + slope2 * (where - past)
                s = jnp.where((where >= low) & (where <= high), s, -1e30)
                s_buf[held(n)] = s
                top[...] = jnp.maximum(top[...], jnp.max(s, axis=0, keepdims=True))

            def weigh(n):
                p = jnp.exp2(s_buf[held(n)] - top[...])
                dp = lax.dot_general(v_all[i, window(n)], g, NT, preferred_element_type=F32)
                s_buf[held(n)] = p
                dp_buf[held(n)] = dp
                low_sum[...] += jnp.sum(p, axis=0, keepdims=True)
                weighted[...] += jnp.sum(p * dp, axis=0, keepdims=True)

            repeat(chunks, score)
            repeat(chunks, weigh)
            share = 1.0 / low_sum[...]
            delta = weighted[...] * share

            def spread(n):
                w = s_buf[held(n)] * share
                ds = (w * (dp_buf[held(n)] - delta)).astype(BF16)
                dv_acc[window(n)] += lax.dot_general(w.astype(BF16), g, NN, preferred_element_type=F32)
                dk_acc[window(n)] += lax.dot_general(ds, q, NN, preferred_element_type=F32)
                dq_acc[...] += lax.dot_general(k_all[i, window(n)], ds, TN, preferred_element_type=F32)

            repeat(chunks, spread)
            dq_mine[i, pl.ds(first, tile)] = (dq_acc[...] * inv_scale).T.astype(BF16)
            return carry

        lax.fori_loop(0, rows // tile, block, 0)
        dk_part[i] = dk_acc[pl.ds(0, past)].astype(BF16)
        dv_part[i] = dv_acc[pl.ds(0, past)].astype(BF16)

    def settle(i, a, acc, scale):
        total = acc
        for r in range(1, reach + 1):
            back_copy(i, a, r).wait_recv()
            total = total + gots[a][i, r - 1].astype(F32)
        mine[1 + a][i] = (total * scale).astype(BF16)
        send_out(i, 1 + a)

    def start_head(i, a):
        for off in offs:
            in_copy(i, a, off).start()
        own_copy(i, a).start()

    def turn(source, target, count):
        if source.shape[0] == tok:
            for n in range(0, tok, count):
                target[:, n : n + count] = jnp.swapaxes(source[n : n + count], 0, 1)
        else:
            for n in range(0, tok, count):
                target[n : n + count] = jnp.swapaxes(source[:, n : n + count], 0, 1)

    step = min(64, tok)
    for a in range(4):
        raw_copy(a).wait()
        turn(raws[a], sources[a], step)
        if a == 0:
            pl.semaphore_wait(barrier, n_head - 1 + 2 * reach)
        start_head(0, a)
    for i in range(1, here):
        for a in range(4):
            start_head(i, a)

    for copy in small:
        copy.wait()
    spots = lax.broadcasted_iota(jnp.int32, (1, rows), 1) + c * rows
    start = jnp.int32(0)
    low = jnp.zeros((1, rows), jnp.int32)
    for n in range(doc_ref.shape[0]):
        low = jnp.where(spots >= start, start, low)
        start = start + doc_ref[n]
    low_ref[...] = (low - c * rows).astype(F32)

    def forward(i):
        for a in range(2):
            arrived(i, a)
            for r in range(1, reach + 1):
                fwd_copy(i, a, r).start()

    forward(0)
    for i in range(here):
        for a in (2, 3):
            arrived(i, a)
        for a in range(2):
            for r in range(1, reach + 1):
                fwd_copy(i, a, r).wait_recv()
        attend(i)
        for a in range(2):
            for r in range(1, reach + 1):
                back_copy(i, a, r).start()
        send_out(i, 0)
        if i + 1 < here:
            forward(i + 1)
        settle(i, 0, dk_acc[pl.ds(past, rows)], inv_scale)
        settle(i, 1, dv_acc[pl.ds(past, rows)], 1.0)

    results = (dq_hbm, dk_hbm, dv_hbm)

    def result_copy(a):
        return pltpu.make_async_copy(raws[a], results[a], raw_sem.at[a])

    for a in range(3):
        for i in range(here):
            for off in offs:
                out_copy(i, a, off).wait_recv()
        turn(outs[a], raws[a], step)
        result_copy(a).start()

    for i in range(here):
        for off in offs:
            for a in range(4):
                in_copy(i, a, off).wait_send()
            for a in range(3):
                out_copy(i, a, off).wait_send()
        for a in range(2):
            for r in range(1, reach + 1):
                fwd_copy(i, a, r).wait_send()
                back_copy(i, a, r).wait_send()
    for a in range(3):
        result_copy(a).wait()


def chain_kernel(
    sizes,
    k_hbm, v_hbm, q_hbm, g_hbm, slope_hbm, doc_hbm,
    dq_out, dk_out, dv_out,
    k_raw, v_raw, q_raw, g_raw, k_in, v_in, q_in, g_in, slope_ref, doc_ref, low_ref,
    k_all, v_all, q_all, g_all,
    p_buf, dp_buf, top, stat, stat_got, both, dq_acc, dk_acc, dv_acc, dq_rows,
    dq_own, dq_next, dq_far, got_next, got_far, got_side, dq_pair, dk_pair, dv_pair, got_pair,
    small_sem, raw_sem, own_sem, in_send, in_recv, near_send, near_recv, far_send, far_recv,
    stat_send, stat_recv, next_send, next_recv, side_recv, back_send, back_recv, pair_send, pair_recv,
):
    n_ctx, mine, tok, depth = sizes
    z = lax.axis_index("head")
    c = lax.axis_index("ctx")
    side = z // 2
    half = lax.rem(z, 2)
    rest = 1 - half
    chunk = 2 * tok
    span = 3 * chunk
    first_key = (2 * c + side) * chunk
    inner = lax.rem(side + half, 2) == 1
    outer = lax.rem(side + half, 2) == 0
    inv_scale = 1.0 / math.sqrt(depth)

    before, after = lax.rem(c - 1 + n_ctx, n_ctx), lax.rem(c + 1, n_ctx)
    c_less = lax.rem(c - (1 - side) + n_ctx, n_ctx)
    c_more = lax.rem(c + side, n_ctx)
    across = z + 2 - 4 * side
    mirror = 3 - z
    twin = {"head": z + 1 - 2 * half}
    less_one, more_one = {"ctx": c_less, "head": across}, {"ctx": c_more, "head": across}
    less_mirror, more_mirror = {"ctx": c_less, "head": mirror}, {"ctx": c_more, "head": mirror}
    less_two, more_two = {"ctx": before}, {"ctx": after}

    def remote(src, dst, send, recv, device):
        return pltpu.make_async_remote_copy(
            src_ref=src, dst_ref=dst, send_sem=send, recv_sem=recv,
            device_id=device, device_id_type=pl.DeviceIdType.MESH,
        )

    wholes = (k_hbm, v_hbm, q_hbm, g_hbm)
    raws = (k_raw, v_raw, q_raw, g_raw)
    sources = (k_in, v_in, q_in, g_in)
    holders = (k_all, v_all, q_all, g_all)

    def raw_copy(a):
        return pltpu.make_async_copy(wholes[a], raws[a], raw_sem.at[a])

    for a in (2, 3, 0, 1):
        raw_copy(a).start()
    small = (
        pltpu.make_async_copy(slope_hbm, slope_ref, small_sem.at[0]),
        pltpu.make_async_copy(doc_hbm, doc_ref, small_sem.at[1]),
    )
    for copy in small:
        copy.start()

    barrier = pltpu.get_barrier_semaphore()

    def greet(device):
        pl.semaphore_signal(barrier, inc=1, device_id=device, device_id_type=pl.DeviceIdType.MESH)

    greet(more_one)
    greet(more_two)
    greet(twin)

    @pl.when(inner)
    def _():
        greet(more_mirror)

    def block(base, which):
        return pl.ds(pl.multiple_of(base + which * tok, tok), tok)

    def own_copy(i, a):
        return pltpu.make_async_copy(sources[a].at[half * mine + i], holders[a].at[i, block(0, half)], own_sem.at[i, a])

    def in_copy(i, a):
        return remote(
            sources[a].at[rest * mine + i], holders[a].at[i, block(0, half)], in_send.at[i, a], in_recv.at[i, a], twin
        )

    def near_own(i, a):
        return remote(
            sources[a].at[half * mine + i], holders[a].at[i, block(chunk, half)],
            near_send.at[i, a - 2, 0], near_recv.at[i, a - 2, half], less_one,
        )

    def near_other(i, a):
        return remote(
            sources[a].at[rest * mine + i], holders[a].at[i, block(chunk, half)],
            near_send.at[i, a - 2, 1], near_recv.at[i, a - 2, half], less_mirror,
        )

    def near_relay(i, a):
        return remote(
            holders[a].at[i, block(0, rest)], holders[a].at[i, block(chunk, rest)],
            near_send.at[i, a - 2, 2], near_recv.at[i, a - 2, rest], less_one,
        )

    def far_copy(i, a):
        return remote(
            holders[a].at[i, pl.ds(0, chunk)], holders[a].at[i, pl.ds(2 * chunk, chunk)],
            far_send.at[i, a - 2], far_recv.at[i, a - 2], less_two,
        )

    routes = (
        (0, less_one, 1, 0),
        (0, less_two, 2, 0),
        (1, more_one, 0, 0),
        (1, less_one, 2, 1),
        (2, more_two, 0, 1),
        (2, more_one, 1, 1),
    )

    def stat_copy(i, m):
        slot, device, there, place = routes[m]
        return remote(
            stat.at[i, slot], stat_got.at[i, there, place], stat_send.at[i, m], stat_recv.at[i, there, place], device
        )

    def next_own(i):
        return remote(
            dq_next.at[i, block(0, half)], got_next.at[i], next_send.at[i, 0], next_recv.at[i], more_one
        )

    def next_side(i):
        kind = lax.rem(side + half + 1, 2)
        device = {"ctx": c_more, "head": 2 - side}
        return remote(
            dq_next.at[i, block(0, rest)], got_side.at[kind, i], next_send.at[i, 1], side_recv.at[kind, i], device
        )

    def back_copy(i):
        return remote(dq_far.at[i], got_far.at[i], back_send.at[i], back_recv.at[i], more_two)

    pairs = (dq_pair, dk_pair, dv_pair)
    pair_targets = (None, dk_out, dv_out)

    def pair_copy(i, a):
        target = got_pair.at[i] if a == 0 else pair_targets[a].at[half * mine + i]
        return remote(pairs[a].at[i], target, pair_send.at[i, a], pair_recv.at[i, a], twin)

    def pair_wait(i, a):
        target = got_pair.at[i] if a == 0 else pair_targets[a].at[rest * mine + i]
        remote(pairs[a].at[i], target, pair_send.at[i, a], pair_recv.at[i, a], twin).wait_recv()

    step = min(64, tok)

    def turn(source, target):
        for n in range(0, tok, step):
            target[:, n : n + step] = jnp.swapaxes(source[n : n + step], 0, 1)

    def open_head(i, a):
        in_copy(i, a).start()
        own_copy(i, a).start()
        if a >= 2:
            near_own(i, a).start()

            @pl.when(inner)
            def _():
                near_other(i, a).start()

    def relay(i):
        for a in (2, 3):
            own_copy(i, a).wait()
            in_copy(i, a).wait_recv()
            far_copy(i, a).start()

            @pl.when(inner)
            def _():
                near_relay(i, a).start()

    def arrived(i):
        for a in (0, 1):
            own_copy(i, a).wait()
            in_copy(i, a).wait_recv()
        for a in (2, 3):
            far_copy(i, a).wait_recv()
            near_own(i, a).wait_recv()
            near_relay(i, a).wait_recv()

    def tile_rows(t):
        return pl.ds(pl.multiple_of(t * tok, tok), tok)

    def gather(i, slot_of):
        slope2 = slope_ref[half * mine + i] * LOG2E

        def slot_step(slot, carry):
            for u in range(2):
                t = 2 * slot + u
                q = q_all[i, tile_rows(t)]
                g = g_all[i, tile_rows(t)]
                low = low_ref[:, tile_rows(t)]
                first = (t * tok).astype(F32)
                high = lax.broadcasted_iota(jnp.int32, (1, tok), 1).astype(F32) + first
                spot = lax.broadcasted_iota(jnp.int32, (tok, tok), 0).astype(F32)
                best = jnp.full((1, tok), -1e30, F32)
                for b in range(2):
                    raw = lax.dot_general(k_all[i, b * tok : (b + 1) * tok], q, NT, preferred_element_type=F32)
                    where = spot + jnp.float32(b * tok)
                    s = raw * (inv_scale * LOG2E) + slope2 * (where - first)
                    s = jnp.where((where >= low) & (where <= high), s, -1e30)
                    p_buf[slot_of, t, b] = s
                    best = jnp.maximum(best, jnp.max(s, axis=0, keepdims=True))
                total = jnp.zeros((1, tok), F32)
                weighted = jnp.zeros((1, tok), F32)
                for b in range(2):
                    p = jnp.exp2(p_buf[slot_of, t, b] - best)
                    dp = lax.dot_general(v_all[i, b * tok : (b + 1) * tok], g, NT, preferred_element_type=F32)
                    p_buf[slot_of, t, b] = p
                    dp_buf[slot_of, t, b] = dp
                    total = total + jnp.sum(p, axis=0, keepdims=True)
                    weighted = weighted + jnp.sum(p * dp, axis=0, keepdims=True)
                top[slot_of, t] = best
                level = best + jnp.log2(total)
                share = weighted / total
                for r in range(lanes):
                    row = u * lanes + r
                    part = slice(r * depth, (r + 1) * depth)
                    stat[i, slot, row : row + 1] = level[:, part]
                    stat[i, slot, 2 * lanes + row : 2 * lanes + row + 1] = share[:, part]
            return carry

        lax.fori_loop(0, 3, slot_step, 0)
        for m in range(6):
            stat_copy(i, m).start()

    lanes = tok // depth

    def spread(i, slot_of):
        for slot in range(3):
            for place in range(2):
                remote(
                    stat.at[i, slot], stat_got.at[i, slot, place], stat_send.at[i, 0], stat_recv.at[i, slot, place], twin
                ).wait_recv()
            found = (stat[i, slot], stat_got[i, slot, 0], stat_got[i, slot, 1])
            levels = [x[: 2 * lanes] for x in found]
            shares = [x[2 * lanes :] for x in found]
            peak = jnp.maximum(jnp.maximum(levels[0], levels[1]), levels[2])
            full = peak + jnp.log2(sum(jnp.exp2(x - peak) for x in levels))
            delta = sum(jnp.exp2(x - full) * y for x, y in zip(levels, shares))
            for u in range(2):
                for r in range(lanes):
                    row = u * lanes + r
                    part = slice(r * depth, (r + 1) * depth)
                    both[0, 2 * slot + u, :, part] = full[row : row + 1]
                    both[1, 2 * slot + u, :, part] = delta[row : row + 1]
        dk_acc[...] = jnp.zeros_like(dk_acc)
        dv_acc[...] = jnp.zeros_like(dv_acc)

        def tile_step(t, carry):
            q = q_all[i, tile_rows(t)]
            g = g_all[i, tile_rows(t)]
            share = jnp.exp2(top[slot_of, t] - both[0, t])
            delta = both[1, t]
            for b in range(2):
                rows = slice(b * tok, (b + 1) * tok)
                w = p_buf[slot_of, t, b] * share
                ds = (w * (dp_buf[slot_of, t, b] - delta)).astype(BF16)
                dv_acc[rows] += lax.dot_general(w.astype(BF16), g, NN, preferred_element_type=F32)
                dk_acc[rows] += lax.dot_general(ds, q, NN, preferred_element_type=F32)
                part = lax.dot_general(k_all[i, rows], ds, TN, preferred_element_type=F32)
                if b == 0:
                    dq_acc[...] = part
                else:
                    dq_acc[...] += part
            dq_rows[tile_rows(t)] = (dq_acc[...] * inv_scale).T
            return carry

        lax.fori_loop(0, 6, tile_step, 0)
        dq_next[i] = dq_rows[chunk : 2 * chunk].astype(BF16)
        dq_far[i] = dq_rows[2 * chunk : 3 * chunk].astype(BF16)
        back_copy(i).start()
        dq_own[i] = dq_rows[0:chunk]
        dk_pair[i] = (dk_acc[block(0, rest)] * inv_scale).astype(BF16)
        pair_copy(i, 1).start()
        dv_pair[i] = dv_acc[block(0, rest)].astype(BF16)
        pair_copy(i, 2).start()
        dk_out[half * mine + i] = (dk_acc[block(0, half)] * inv_scale).astype(BF16)
        dv_out[half * mine + i] = dv_acc[block(0, half)].astype(BF16)

    def send_next(i):
        next_side(i).start()
        next_own(i).start()

    def settle(i):
        back_copy(i).wait_recv()

        @pl.when(inner)
        def _():
            remote(dq_pair.at[i], got_side.at[1, i], next_send.at[i, 1], side_recv.at[1, i], twin).wait_recv()

        dq_pair[i] = (
            dq_own[i, block(0, rest)] + got_far[i, block(0, rest)].astype(F32) + got_side[1, i].astype(F32)
        ).astype(BF16)
        pair_copy(i, 0).start()
        next_own(i).wait_recv()
        dq_out[half * mine + i] = (
            dq_own[i, block(0, half)] + got_far[i, block(0, half)].astype(F32) + got_next[i].astype(F32)
        ).astype(BF16)

    def close(i):
        pair_wait(i, 0)

        @pl.when(inner)
        def _():
            remote(dq_pair.at[i], got_side.at[0, i], next_send.at[i, 1], side_recv.at[0, i], twin).wait_recv()

        dq_out[rest * mine + i] = (got_pair[i].astype(F32) + got_side[0, i].astype(F32)).astype(BF16)

    for a in (2, 3, 0, 1):
        raw_copy(a).wait()
        turn(raws[a], sources[a])
        if a == 2:
            pl.semaphore_wait(barrier, 3 + lax.rem(side + half, 2))
        open_head(0, a)
    for a in (2, 3, 0, 1):
        if mine > 1:
            open_head(1, a)

    @pl.when(outer)
    def _():
        got_side[...] = jnp.zeros_like(got_side)

    for copy in small:
        copy.wait()
    spots = lax.broadcasted_iota(jnp.int32, (1, span), 1) + first_key
    start = jnp.int32(0)
    low = jnp.zeros((1, span), jnp.int32)
    for n in range(doc_ref.shape[0]):
        low = jnp.where(spots >= start, start, low)
        start = start + doc_ref[n]
    low = jnp.where(spots >= start, spots + 1, low)
    low_ref[...] = (low - first_key).astype(F32)

    relay(0)
    if mine > 1:
        relay(1)
    held = []
    for i in range(mine):
        if i + 2 < mine:
            for a in (2, 3, 0, 1):
                open_head(i + 2, a)
        arrived(i)
        gather(i, i % 2)
        for m in held:
            send_next(m)
        held = []
        if i >= 1:
            spread(i - 1, (i - 1) % 2)
            held = [i - 1]
        if i + 2 < mine:
            relay(i + 2)
        if i + 3 >= mine and i + 1 < mine and i + 2 < mine:
            for m in held:
                send_next(m)
            held = []
    for m in held:
        send_next(m)
    spread(mine - 1, (mine - 1) % 2)
    send_next(mine - 1)
    for i in range(mine):
        settle(i)

    for a in (1, 2):
        for i in range(mine):
            pair_wait(i, a)
    for i in range(mine):
        close(i)

    for i in range(mine):
        for a in range(4):
            in_copy(i, a).wait_send()
        for a in (2, 3):
            near_own(i, a).wait_send()
            far_copy(i, a).wait_send()
        for m in range(6):
            stat_copy(i, m).wait_send()
        next_own(i).wait_send()
        next_side(i).wait_send()
        back_copy(i).wait_send()
        for a in range(3):
            pair_copy(i, a).wait_send()

    @pl.when(inner)
    def _():
        for i in range(mine):
            for a in (2, 3):
                near_other(i, a).wait_send()
                near_relay(i, a).wait_send()


def chain_call(n_ctx, tok, heads, depth, slots, docs):
    mine = heads // 2
    chunk = 2 * tok
    away = pl.BlockSpec(memory_space=pltpu.MemorySpace.HBM)
    dma = pltpu.SemaphoreType.DMA
    out = jax.ShapeDtypeStruct((heads, tok, depth), BF16)
    near = pl.BlockSpec(memory_space=pltpu.VMEM)
    pairs = mine * 6 * chunk * tok
    return pl.pallas_call(
        partial(chain_kernel, (n_ctx, mine, tok, depth)),
        out_shape=(out, out, out),
        in_specs=[away] * 6,
        out_specs=(near,) * 3,
        scratch_shapes=[pltpu.VMEM((tok, heads, depth), BF16)] * 4
        + [pltpu.VMEM((heads, tok, depth), BF16)] * 4
        + [
            pltpu.SMEM(slots, F32),
            pltpu.SMEM(docs, jnp.int32),
            pltpu.VMEM((1, 3 * chunk), F32),
            pltpu.VMEM((mine, chunk, depth), BF16),
            pltpu.VMEM((mine, chunk, depth), BF16),
            pltpu.VMEM((mine, 3 * chunk, depth), BF16),
            pltpu.VMEM((mine, 3 * chunk, depth), BF16),
            pltpu.VMEM((2, 6, 2, tok, tok), F32),
            pltpu.VMEM((2, 6, 2, tok, tok), F32),
            pltpu.VMEM((2, 6, 1, tok), F32),
            pltpu.VMEM((mine, 3, 4 * tok // depth, depth), F32),
            pltpu.VMEM((mine, 3, 2, 4 * tok // depth, depth), F32),
            pltpu.VMEM((2, 6, 1, tok), F32),
            pltpu.VMEM((depth, tok), F32),
            pltpu.VMEM((chunk, depth), F32),
            pltpu.VMEM((chunk, depth), F32),
            pltpu.VMEM((3 * chunk, depth), F32),
            pltpu.VMEM((mine, chunk, depth), F32),
            pltpu.VMEM((mine, chunk, depth), BF16),
            pltpu.VMEM((mine, chunk, depth), BF16),
            pltpu.VMEM((mine, tok, depth), BF16),
            pltpu.VMEM((mine, chunk, depth), BF16),
            pltpu.VMEM((2, mine, tok, depth), BF16),
            pltpu.VMEM((mine, tok, depth), BF16),
            pltpu.VMEM((mine, tok, depth), BF16),
            pltpu.VMEM((mine, tok, depth), BF16),
            pltpu.VMEM((mine, tok, depth), BF16),
            dma((2,)),
            dma((4,)),
            dma((mine, 4)),
            dma((mine, 4)),
            dma((mine, 4)),
            dma((mine, 2, 3)),
            dma((mine, 2, 2)),
            dma((mine, 2)),
            dma((mine, 2)),
            dma((mine, 6)),
            dma((mine, 3, 2)),
            dma((mine, 2)),
            dma((mine,)),
            dma((2, mine)),
            dma((mine,)),
            dma((mine,)),
            dma((mine, 3)),
            dma((mine, 3)),
        ],
        compiler_params=pltpu.CompilerParams(
            collective_id=1, has_side_effects=True, vmem_limit_bytes=VMEM_PART
        ),
        cost_estimate=pl.CostEstimate(
            flops=10 * pairs * depth, bytes_accessed=14 * heads * tok * depth, transcendentals=pairs
        ),
    )


def turn_over(a_in, b_in, c_in, a_out, b_out, c_out, a_buf, b_buf, c_buf, sem):
    tok = a_buf.shape[0]
    step = min(64, tok)
    copies = []
    for m, (x, buf, y) in enumerate(((b_in, b_buf, b_out), (c_in, c_buf, c_out), (a_in, a_buf, a_out))):
        for n in range(0, tok, step):
            buf[n : n + step] = jnp.swapaxes(x[:, n : n + step], 0, 1)
        copies.append(pltpu.make_async_copy(buf, y, sem.at[m]))
        copies[-1].start()
    for copy in copies:
        copy.wait()


def hand_over(a_in, b_in, c_in, a_out, b_out, c_out, a_buf, b_buf, c_buf, in_sem, out_sem):
    bufs = (a_buf, b_buf, c_buf)
    ins = [pltpu.make_async_copy(x, bufs[n], in_sem.at[n]) for n, x in enumerate((a_in, b_in, c_in))]
    outs = [pltpu.make_async_copy(bufs[n], x, out_sem.at[n]) for n, x in enumerate((a_out, b_out, c_out))]
    for copy in ins:
        copy.start()
    for arrive, leave in zip(ins, outs):
        arrive.wait()
        leave.start()
    for copy in outs:
        copy.wait()


def stay(x):
    return pltpu.with_memory_space_constraint(x, pltpu.MemorySpace.HBM)


def body(queries, keys_in, values, grad_out, slopes, doc_lengths):
    n_head = lax.axis_size("head")
    n_ctx = lax.axis_size("ctx")
    tok, heads, depth = queries.shape
    here = heads // n_head
    rows = tok * n_head
    span = min(16384, rows * n_ctx // 8)
    reach = span // rows
    past = reach * rows
    tile = min(256, rows)
    sizes = (n_head, n_ctx, reach, here, tok, rows, depth, tile)
    away = pl.BlockSpec(memory_space=pl.ANY)
    dma = pltpu.SemaphoreType.DMA
    out = jax.ShapeDtypeStruct((tok, heads, depth), BF16)
    swapped = pltpu.VMEM((heads, tok, depth), BF16)
    window = past + tile
    pairs = rows * window * here
    call = pl.pallas_call(
        partial(kernel, sizes),
        out_shape=(out, out, out),
        in_specs=[away] * 6,
        out_specs=(away,) * 3,
        scratch_shapes=[pltpu.VMEM((tok, heads, depth), BF16)] * 4
        + [swapped] * 7
        + [
            pltpu.SMEM(slopes.shape, F32),
            pltpu.SMEM(doc_lengths.shape, jnp.int32),
            pltpu.VMEM((1, rows), F32),
            pltpu.VMEM((here, past + rows, depth), BF16),
            pltpu.VMEM((here, past + rows, depth), BF16),
            pltpu.VMEM((here, rows, depth), BF16),
            pltpu.VMEM((here, rows, depth), BF16),
            pltpu.VMEM((window, tile), F32),
            pltpu.VMEM((window, tile), F32),
            pltpu.VMEM((1, tile), F32),
            pltpu.VMEM((1, tile), F32),
            pltpu.VMEM((1, tile), F32),
            pltpu.VMEM((depth, tile), F32),
            pltpu.VMEM((past + rows, depth), F32),
            pltpu.VMEM((past + rows, depth), F32),
            pltpu.VMEM((here, rows, depth), BF16),
            pltpu.VMEM((here, rows, depth), BF16),
            pltpu.VMEM((here, rows, depth), BF16),
            pltpu.VMEM((here, past, depth), BF16),
            pltpu.VMEM((here, past, depth), BF16),
            pltpu.VMEM((here, reach, rows, depth), BF16),
            pltpu.VMEM((here, reach, rows, depth), BF16),
            dma((2,)),
            dma((4,)),
            dma((here, 4)),
            dma((here, 4, n_head - 1)),
            dma((here, 4, n_head - 1)),
            dma((here, 2, reach)),
            dma((here, 2, reach)),
            dma((here, 2, reach)),
            dma((here, 2, reach)),
            dma((here, 3, n_head - 1)),
            dma((here, 3, n_head - 1)),
        ],
        compiler_params=pltpu.CompilerParams(
            collective_id=0, has_side_effects=True, vmem_limit_bytes=VMEM_ALL
        ),
        cost_estimate=pl.CostEstimate(
            flops=10 * pairs * depth, bytes_accessed=14 * heads * tok * depth, transcendentals=pairs
        ),
    )
    if n_head == 4 and past == rows and heads % 2 == 0 and tok % (2 * depth) == 0:
        call = chain_call(n_ctx, tok, heads, depth, slopes.shape, doc_lengths.shape)
        near = pl.BlockSpec(memory_space=pltpu.VMEM)
        return pl.pallas_call(
            turn_over,
            out_shape=(out, out, out),
            in_specs=[near] * 3,
            out_specs=(away,) * 3,
            scratch_shapes=[pltpu.VMEM((tok, heads, depth), BF16)] * 3 + [dma((3,))],
            compiler_params=pltpu.CompilerParams(vmem_limit_bytes=VMEM_PART),
        )(*call(*(stay(x) for x in (keys_in, values, queries, grad_out, slopes, doc_lengths))))
    grads = call(keys_in, values, queries, grad_out, slopes, doc_lengths)
    return pl.pallas_call(
        hand_over,
        out_shape=(out, out, out),
        in_specs=[away] * 3,
        out_specs=(away,) * 3,
        scratch_shapes=[pltpu.VMEM((tok, heads, depth), BF16)] * 3 + [dma((3,)), dma((3,))],
        compiler_params=pltpu.CompilerParams(vmem_limit_bytes=VMEM_ALL),
    )(*grads)


def solution(mesh):
    placed = P(("ctx", "head"), None, None)
    return jax.shard_map(
        body,
        mesh=mesh,
        in_specs=(placed, placed, placed, placed, P(), P()),
        out_specs=(placed, placed, placed),
        check_vma=False,
    )
```

```python
from functools import partial
import math

import jax
import jax.numpy as jnp
from jax import lax
from jax.experimental import pallas as pl
from jax.experimental.pallas import tpu as pltpu
from jax.sharding import PartitionSpec as P

F32 = jnp.float32
BF16 = jnp.bfloat16
VMEM_ALL = 65208320
VMEM_PART = 48 << 20
LOG2E = math.log2(math.e)
NT = (((1,), (1,)), ((), ()))
NN = (((1,), (0,)), ((), ()))
TN = (((0,), (0,)), ((), ()))


def repeat(count, step):
    if count <= 8:
        for n in range(count):
            step(n)
    else:

        def looped(n, carry):
            step(n)
            return carry

        lax.fori_loop(0, count, looped, 0)


def kernel(
    sizes,
    k_hbm, v_hbm, q_hbm, g_hbm, slope_hbm, doc_hbm,
    dq_hbm, dk_hbm, dv_hbm,
    k_raw, v_raw, q_raw, g_raw, k_in, v_in, q_in, g_in, dq_out, dk_out, dv_out, slope_ref, doc_ref, low_ref,
    k_all, v_all, q_all, g_all,
    s_buf, dp_buf, top, low_sum, weighted, dq_acc, dk_acc, dv_acc,
    dq_mine, dk_mine, dv_mine, dk_part, dv_part, dk_got, dv_got,
    small_sem, raw_sem, own_sem, in_send, in_recv, fwd_send, fwd_recv, back_send, back_recv, out_send, out_recv,
):
    n_head, n_ctx, reach, here, tok, rows, depth, tile = sizes
    z = lax.axis_index("head")
    c = lax.axis_index("ctx")
    past = reach * rows
    chunks = (past + tile) // tile
    inv_scale = 1.0 / math.sqrt(depth)

    def peer(off):
        other, bit = z, 1
        while bit < n_head:
            if off & bit:
                other = other + bit * (1 - 2 * lax.rem(z // bit, 2))
            bit *= 2
        return other

    offs = tuple(range(1, n_head))

    def along(off):
        return lax.rem(c + off + n_ctx, n_ctx)

    wholes = (k_hbm, v_hbm, q_hbm, g_hbm)
    raws = (k_raw, v_raw, q_raw, g_raw)

    def raw_copy(a):
        return pltpu.make_async_copy(wholes[a], raws[a], raw_sem.at[a])

    for a in range(4):
        raw_copy(a).start()
    small = (
        pltpu.make_async_copy(slope_hbm, slope_ref, small_sem.at[0]),
        pltpu.make_async_copy(doc_hbm, doc_ref, small_sem.at[1]),
    )
    for copy in small:
        copy.start()

    barrier = pltpu.get_barrier_semaphore()
    for off in range(1, n_head):
        pl.semaphore_signal(barrier, inc=1, device_id={"head": peer(off)}, device_id_type=pl.DeviceIdType.MESH)
    for off in range(1, reach + 1):
        for side in (off, -off):
            pl.semaphore_signal(barrier, inc=1, device_id={"ctx": along(side)}, device_id_type=pl.DeviceIdType.MESH)

    sources = (k_in, v_in, q_in, g_in)
    holders = (k_all, v_all, q_all, g_all)
    bases = (past, past, 0, 0)

    def own_copy(i, a):
        return pltpu.make_async_copy(
            sources[a].at[z * here + i],
            holders[a].at[i, pl.ds(pl.multiple_of(bases[a] + z * tok, tok), tok)],
            own_sem.at[i, a],
        )

    def in_copy(i, a, off):
        return pltpu.make_async_remote_copy(
            src_ref=sources[a].at[peer(off) * here + i],
            dst_ref=holders[a].at[i, pl.ds(pl.multiple_of(bases[a] + z * tok, tok), tok)],
            send_sem=in_send.at[i, a, off - 1],
            recv_sem=in_recv.at[i, a, off - 1],
            device_id={"head": peer(off)},
            device_id_type=pl.DeviceIdType.MESH,
        )

    def fwd_copy(i, a, r):
        return pltpu.make_async_remote_copy(
            src_ref=holders[a].at[i, pl.ds(past, rows)],
            dst_ref=holders[a].at[i, pl.ds((reach - r) * rows, rows)],
            send_sem=fwd_send.at[i, a, r - 1],
            recv_sem=fwd_recv.at[i, a, r - 1],
            device_id={"ctx": along(r)},
            device_id_type=pl.DeviceIdType.MESH,
        )

    parts = (dk_part, dv_part)
    gots = (dk_got, dv_got)

    def back_copy(i, a, r):
        return pltpu.make_async_remote_copy(
            src_ref=parts[a].at[i, pl.ds((reach - r) * rows, rows)],
            dst_ref=gots[a].at[i, r - 1],
            send_sem=back_send.at[i, a, r - 1],
            recv_sem=back_recv.at[i, a, r - 1],
            device_id={"ctx": along(-r)},
            device_id_type=pl.DeviceIdType.MESH,
        )

    mine = (dq_mine, dk_mine, dv_mine)
    outs = (dq_out, dk_out, dv_out)

    def out_copy(i, a, off):
        return pltpu.make_async_remote_copy(
            src_ref=mine[a].at[i, pl.ds(pl.multiple_of(peer(off) * tok, tok), tok)],
            dst_ref=outs[a].at[z * here + i],
            send_sem=out_send.at[i, a, off - 1],
            recv_sem=out_recv.at[i, a, off - 1],
            device_id={"head": peer(off)},
            device_id_type=pl.DeviceIdType.MESH,
        )

    def send_out(i, a):
        for off in offs:
            out_copy(i, a, off).start()
        outs[a][z * here + i] = mine[a][i, pl.ds(pl.multiple_of(z * tok, tok), tok)]

    def arrived(i, a):
        own_copy(i, a).wait()
        for off in range(1, n_head):
            in_copy(i, a, off).wait_recv()

    def attend(i):
        slope2 = slope_ref[z * here + i] * LOG2E
        dk_acc[...] = jnp.zeros_like(dk_acc)
        dv_acc[...] = jnp.zeros_like(dv_acc)

        def block(b, carry):
            first = pl.multiple_of(b * tile, tile)
            q = q_all[i, pl.ds(first, tile)]
            g = g_all[i, pl.ds(first, tile)]
            low = low_ref[:, pl.ds(first, tile)] + (past - first).astype(F32)
            high = past + lax.broadcasted_iota(jnp.int32, (1, tile), 1)
            high = high.astype(F32)
            spot = lax.broadcasted_iota(jnp.int32, (tile, tile), 0).astype(F32)
            top[...] = jnp.full_like(top, -1e30)
            low_sum[...] = jnp.zeros_like(low_sum)
            weighted[...] = jnp.zeros_like(weighted)
            dq_acc[...] = jnp.zeros_like(dq_acc)

            def window(n):
                return pl.ds(pl.multiple_of(first + n * tile, tile), tile)

            def held(n):
                return pl.ds(pl.multiple_of(n * tile, tile), tile)

            def score(n):
                raw = lax.dot_general(k_all[i, window(n)], q, NT, preferred_element_type=F32)
                where = spot + jnp.float32(n * tile)
                s = raw * (inv_scale * LOG2E) + slope2 * (where - past)
                s = jnp.where((where >= low) & (where <= high), s, -1e30)
                s_buf[held(n)] = s
                top[...] = jnp.maximum(top[...], jnp.max(s, axis=0, keepdims=True))

            def weigh(n):
                p = jnp.exp2(s_buf[held(n)] - top[...])
                dp = lax.dot_general(v_all[i, window(n)], g, NT, preferred_element_type=F32)
                s_buf[held(n)] = p
                dp_buf[held(n)] = dp
                low_sum[...] += jnp.sum(p, axis=0, keepdims=True)
                weighted[...] += jnp.sum(p * dp, axis=0, keepdims=True)

            repeat(chunks, score)
            repeat(chunks, weigh)
            share = 1.0 / low_sum[...]
            delta = weighted[...] * share

            def spread(n):
                w = s_buf[held(n)] * share
                ds = (w * (dp_buf[held(n)] - delta)).astype(BF16)
                dv_acc[window(n)] += lax.dot_general(w.astype(BF16), g, NN, preferred_element_type=F32)
                dk_acc[window(n)] += lax.dot_general(ds, q, NN, preferred_element_type=F32)
                dq_acc[...] += lax.dot_general(k_all[i, window(n)], ds, TN, preferred_element_type=F32)

            repeat(chunks, spread)
            dq_mine[i, pl.ds(first, tile)] = (dq_acc[...] * inv_scale).T.astype(BF16)
            return carry

        lax.fori_loop(0, rows // tile, block, 0)
        dk_part[i] = dk_acc[pl.ds(0, past)].astype(BF16)
        dv_part[i] = dv_acc[pl.ds(0, past)].astype(BF16)

    def settle(i, a, acc, scale):
        total = acc
        for r in range(1, reach + 1):
            back_copy(i, a, r).wait_recv()
            total = total + gots[a][i, r - 1].astype(F32)
        mine[1 + a][i] = (total * scale).astype(BF16)
        send_out(i, 1 + a)

    def start_head(i, a):
        for off in offs:
            in_copy(i, a, off).start()
        own_copy(i, a).start()

    def turn(source, target, count):
        if source.shape[0] == tok:
            for n in range(0, tok, count):
                target[:, n : n + count] = jnp.swapaxes(source[n : n + count], 0, 1)
        else:
            for n in range(0, tok, count):
                target[n : n + count] = jnp.swapaxes(source[:, n : n + count], 0, 1)

    step = min(64, tok)
    for a in range(4):
        raw_copy(a).wait()
        turn(raws[a], sources[a], step)
        if a == 0:
            pl.semaphore_wait(barrier, n_head - 1 + 2 * reach)
        start_head(0, a)
    for i in range(1, here):
        for a in range(4):
            start_head(i, a)

    for copy in small:
        copy.wait()
    spots = lax.broadcasted_iota(jnp.int32, (1, rows), 1) + c * rows
    start = jnp.int32(0)
    low = jnp.zeros((1, rows), jnp.int32)
    for n in range(doc_ref.shape[0]):
        low = jnp.where(spots >= start, start, low)
        start = start + doc_ref[n]
    low_ref[...] = (low - c * rows).astype(F32)

    def forward(i):
        for a in range(2):
            arrived(i, a)
            for r in range(1, reach + 1):
                fwd_copy(i, a, r).start()

    forward(0)
    for i in range(here):
        for a in (2, 3):
            arrived(i, a)
        for a in range(2):
            for r in range(1, reach + 1):
                fwd_copy(i, a, r).wait_recv()
        attend(i)
        for a in range(2):
            for r in range(1, reach + 1):
                back_copy(i, a, r).start()
        send_out(i, 0)
        if i + 1 < here:
            forward(i + 1)
        settle(i, 0, dk_acc[pl.ds(past, rows)], inv_scale)
        settle(i, 1, dv_acc[pl.ds(past, rows)], 1.0)

    results = (dq_hbm, dk_hbm, dv_hbm)

    def result_copy(a):
        return pltpu.make_async_copy(raws[a], results[a], raw_sem.at[a])

    for a in range(3):
        for i in range(here):
            for off in offs:
                out_copy(i, a, off).wait_recv()
        turn(outs[a], raws[a], step)
        result_copy(a).start()

    for i in range(here):
        for off in offs:
            for a in range(4):
                in_copy(i, a, off).wait_send()
            for a in range(3):
                out_copy(i, a, off).wait_send()
        for a in range(2):
            for r in range(1, reach + 1):
                fwd_copy(i, a, r).wait_send()
                back_copy(i, a, r).wait_send()
    for a in range(3):
        result_copy(a).wait()


def chain_kernel(
    sizes,
    k_hbm, v_hbm, q_hbm, g_hbm, slope_hbm, doc_hbm,
    dq_out, dk_out, dv_out,
    k_raw, v_raw, q_raw, g_raw, k_in, v_in, q_in, g_in, slope_ref, doc_ref, low_ref,
    k_all, v_all, q_all, g_all,
    p_buf, dp_buf, top, stat, stat_got, both, dq_acc, dk_acc, dv_acc, dq_rows,
    dq_own, dq_next, dq_far, got_next, got_far, got_side, dq_pair, dk_pair, dv_pair, got_pair,
    small_sem, raw_sem, own_sem, in_send, in_recv, near_send, near_recv, far_send, far_recv,
    stat_send, stat_recv, next_send, next_recv, side_recv, back_send, back_recv, pair_send, pair_recv,
):
    n_ctx, mine, tok, depth = sizes
    z = lax.axis_index("head")
    c = lax.axis_index("ctx")
    side = z // 2
    half = lax.rem(z, 2)
    rest = 1 - half
    chunk = 2 * tok
    span = 3 * chunk
    first_key = (2 * c + side) * chunk
    inner = lax.rem(side + half, 2) == 1
    outer = lax.rem(side + half, 2) == 0
    inv_scale = 1.0 / math.sqrt(depth)

    before, after = lax.rem(c - 1 + n_ctx, n_ctx), lax.rem(c + 1, n_ctx)
    c_less = lax.rem(c - (1 - side) + n_ctx, n_ctx)
    c_more = lax.rem(c + side, n_ctx)
    across = z + 2 - 4 * side
    mirror = 3 - z
    twin = {"head": z + 1 - 2 * half}
    less_one, more_one = {"ctx": c_less, "head": across}, {"ctx": c_more, "head": across}
    less_mirror, more_mirror = {"ctx": c_less, "head": mirror}, {"ctx": c_more, "head": mirror}
    less_two, more_two = {"ctx": before}, {"ctx": after}

    def remote(src, dst, send, recv, device):
        return pltpu.make_async_remote_copy(
            src_ref=src, dst_ref=dst, send_sem=send, recv_sem=recv,
            device_id=device, device_id_type=pl.DeviceIdType.MESH,
        )

    wholes = (k_hbm, v_hbm, q_hbm, g_hbm)
    raws = (k_raw, v_raw, q_raw, g_raw)
    sources = (k_in, v_in, q_in, g_in)
    holders = (k_all, v_all, q_all, g_all)

    def raw_copy(a):
        return pltpu.make_async_copy(wholes[a], raws[a], raw_sem.at[a])

    for a in (2, 3, 0, 1):
        raw_copy(a).start()
    small = (
        pltpu.make_async_copy(slope_hbm, slope_ref, small_sem.at[0]),
        pltpu.make_async_copy(doc_hbm, doc_ref, small_sem.at[1]),
    )
    for copy in small:
        copy.start()

    barrier = pltpu.get_barrier_semaphore()

    def greet(device):
        pl.semaphore_signal(barrier, inc=1, device_id=device, device_id_type=pl.DeviceIdType.MESH)

    greet(more_one)
    greet(more_two)
    greet(twin)

    @pl.when(inner)
    def _():
        greet(more_mirror)

    def block(base, which):
        return pl.ds(pl.multiple_of(base + which * tok, tok), tok)

    def own_copy(i, a):
        return pltpu.make_async_copy(sources[a].at[half * mine + i], holders[a].at[i, block(0, half)], own_sem.at[i, a])

    def in_copy(i, a):
        return remote(
            sources[a].at[rest * mine + i], holders[a].at[i, block(0, half)], in_send.at[i, a], in_recv.at[i, a], twin
        )

    def near_own(i, a):
        return remote(
            sources[a].at[half * mine + i], holders[a].at[i, block(chunk, half)],
            near_send.at[i, a - 2, 0], near_recv.at[i, a - 2, half], less_one,
        )

    def near_other(i, a):
        return remote(
            sources[a].at[rest * mine + i], holders[a].at[i, block(chunk, half)],
            near_send.at[i, a - 2, 1], near_recv.at[i, a - 2, half], less_mirror,
        )

    def near_relay(i, a):
        return remote(
            holders[a].at[i, block(0, rest)], holders[a].at[i, block(chunk, rest)],
            near_send.at[i, a - 2, 2], near_recv.at[i, a - 2, rest], less_one,
        )

    def far_copy(i, a):
        return remote(
            holders[a].at[i, pl.ds(0, chunk)], holders[a].at[i, pl.ds(2 * chunk, chunk)],
            far_send.at[i, a - 2], far_recv.at[i, a - 2], less_two,
        )

    routes = (
        (0, less_one, 1, 0),
        (0, less_two, 2, 0),
        (1, more_one, 0, 0),
        (1, less_one, 2, 1),
        (2, more_two, 0, 1),
        (2, more_one, 1, 1),
    )

    def stat_copy(i, m):
        slot, device, there, place = routes[m]
        return remote(
            stat.at[i, slot], stat_got.at[i, there, place], stat_send.at[i, m], stat_recv.at[i, there, place], device
        )

    def next_own(i):
        return remote(
            dq_next.at[i, block(0, half)], got_next.at[i], next_send.at[i, 0], next_recv.at[i], more_one
        )

    def next_side(i):
        if i == mine - 1:
            return remote(
                dq_next.at[i, block(0, rest)], got_side.at[0, i], next_send.at[i, 1], side_recv.at[0, i], more_mirror
            )
        kind = lax.rem(side + half + 1, 2)
        device = {"ctx": c_more, "head": 2 - side}
        return remote(
            dq_next.at[i, block(0, rest)], got_side.at[kind, i], next_send.at[i, 1], side_recv.at[kind, i], device
        )

    def back_copy(i):
        return remote(dq_far.at[i], got_far.at[i], back_send.at[i], back_recv.at[i], more_two)

    pairs = (dq_pair, dk_pair, dv_pair)
    pair_targets = (None, dk_out, dv_out)

    def pair_copy(i, a):
        target = got_pair.at[i] if a == 0 else pair_targets[a].at[half * mine + i]
        return remote(pairs[a].at[i], target, pair_send.at[i, a], pair_recv.at[i, a], twin)

    def pair_wait(i, a):
        target = got_pair.at[i] if a == 0 else pair_targets[a].at[rest * mine + i]
        remote(pairs[a].at[i], target, pair_send.at[i, a], pair_recv.at[i, a], twin).wait_recv()

    step = min(64, tok)

    def turn(source, target):
        for n in range(0, tok, step):
            target[:, n : n + step] = jnp.swapaxes(source[n : n + step], 0, 1)

    def open_head(i, a):
        in_copy(i, a).start()
        own_copy(i, a).start()
        if a >= 2:
            near_own(i, a).start()

            @pl.when(inner)
            def _():
                near_other(i, a).start()

    def relay(i):
        for a in (2, 3):
            own_copy(i, a).wait()
            in_copy(i, a).wait_recv()
            far_copy(i, a).start()

            @pl.when(inner)
            def _():
                near_relay(i, a).start()

    def arrived(i):
        for a in (0, 1):
            own_copy(i, a).wait()
            in_copy(i, a).wait_recv()
        for a in (2, 3):
            far_copy(i, a).wait_recv()
            near_own(i, a).wait_recv()
            near_relay(i, a).wait_recv()

    def tile_rows(t):
        return pl.ds(pl.multiple_of(t * tok, tok), tok)

    def gather(i, slot_of):
        slope2 = slope_ref[half * mine + i] * LOG2E

        def slot_step(slot, carry):
            for u in range(2):
                t = 2 * slot + u
                q = q_all[i, tile_rows(t)]
                g = g_all[i, tile_rows(t)]
                low = low_ref[:, tile_rows(t)]
                first = (t * tok).astype(F32)
                high = lax.broadcasted_iota(jnp.int32, (1, tok), 1).astype(F32) + first
                spot = lax.broadcasted_iota(jnp.int32, (tok, tok), 0).astype(F32)
                best = jnp.full((1, tok), -1e30, F32)
                for b in range(2):
                    raw = lax.dot_general(k_all[i, b * tok : (b + 1) * tok], q, NT, preferred_element_type=F32)
                    where = spot + jnp.float32(b * tok)
                    s = raw * (inv_scale * LOG2E) + slope2 * (where - first)
                    s = jnp.where((where >= low) & (where <= high), s, -1e30)
                    p_buf[slot_of, t, b] = s
                    best = jnp.maximum(best, jnp.max(s, axis=0, keepdims=True))
                total = jnp.zeros((1, tok), F32)
                weighted = jnp.zeros((1, tok), F32)
                for b in range(2):
                    p = jnp.exp2(p_buf[slot_of, t, b] - best)
                    dp = lax.dot_general(v_all[i, b * tok : (b + 1) * tok], g, NT, preferred_element_type=F32)
                    p_buf[slot_of, t, b] = p
                    dp_buf[slot_of, t, b] = dp
                    total = total + jnp.sum(p, axis=0, keepdims=True)
                    weighted = weighted + jnp.sum(p * dp, axis=0, keepdims=True)
                top[slot_of, t] = best
                level = best + jnp.log2(total)
                share = weighted / total
                for r in range(lanes):
                    row = u * lanes + r
                    part = slice(r * depth, (r + 1) * depth)
                    stat[i, slot, row : row + 1] = level[:, part]
                    stat[i, slot, 2 * lanes + row : 2 * lanes + row + 1] = share[:, part]
            return carry

        lax.fori_loop(0, 3, slot_step, 0)
        for m in range(6):
            stat_copy(i, m).start()

    lanes = tok // depth

    def spread(i, slot_of):
        for slot in range(3):
            for place in range(2):
                remote(
                    stat.at[i, slot], stat_got.at[i, slot, place], stat_send.at[i, 0], stat_recv.at[i, slot, place], twin
                ).wait_recv()
            found = (stat[i, slot], stat_got[i, slot, 0], stat_got[i, slot, 1])
            levels = [x[: 2 * lanes] for x in found]
            shares = [x[2 * lanes :] for x in found]
            peak = jnp.maximum(jnp.maximum(levels[0], levels[1]), levels[2])
            full = peak + jnp.log2(sum(jnp.exp2(x - peak) for x in levels))
            delta = sum(jnp.exp2(x - full) * y for x, y in zip(levels, shares))
            for u in range(2):
                for r in range(lanes):
                    row = u * lanes + r
                    part = slice(r * depth, (r + 1) * depth)
                    both[0, 2 * slot + u, :, part] = full[row : row + 1]
                    both[1, 2 * slot + u, :, part] = delta[row : row + 1]
        dk_acc[...] = jnp.zeros_like(dk_acc)
        dv_acc[...] = jnp.zeros_like(dv_acc)

        def tile_step(t, carry):
            q = q_all[i, tile_rows(t)]
            g = g_all[i, tile_rows(t)]
            share = jnp.exp2(top[slot_of, t] - both[0, t])
            delta = both[1, t]
            for b in range(2):
                rows = slice(b * tok, (b + 1) * tok)
                w = p_buf[slot_of, t, b] * share
                ds = (w * (dp_buf[slot_of, t, b] - delta)).astype(BF16)
                dv_acc[rows] += lax.dot_general(w.astype(BF16), g, NN, preferred_element_type=F32)
                dk_acc[rows] += lax.dot_general(ds, q, NN, preferred_element_type=F32)
                part = lax.dot_general(k_all[i, rows], ds, TN, preferred_element_type=F32)
                if b == 0:
                    dq_acc[...] = part
                else:
                    dq_acc[...] += part
            dq_rows[tile_rows(t)] = (dq_acc[...] * inv_scale).T
            return carry

        lax.fori_loop(0, 6, tile_step, 0)
        dq_next[i] = dq_rows[chunk : 2 * chunk].astype(BF16)
        dq_far[i] = dq_rows[2 * chunk : 3 * chunk].astype(BF16)
        back_copy(i).start()
        dq_own[i] = dq_rows[0:chunk]
        dk_pair[i] = (dk_acc[block(0, rest)] * inv_scale).astype(BF16)
        pair_copy(i, 1).start()
        dv_pair[i] = dv_acc[block(0, rest)].astype(BF16)
        pair_copy(i, 2).start()
        dk_out[half * mine + i] = (dk_acc[block(0, half)] * inv_scale).astype(BF16)
        dv_out[half * mine + i] = dv_acc[block(0, half)].astype(BF16)

    def send_next(i):
        next_side(i).start()
        next_own(i).start()

    def settle(i):
        back_copy(i).wait_recv()
        passed = dq_own[i, block(0, rest)] + got_far[i, block(0, rest)].astype(F32)
        if i < mine - 1:

            @pl.when(inner)
            def _():
                remote(dq_pair.at[i], got_side.at[1, i], next_send.at[i, 1], side_recv.at[1, i], twin).wait_recv()

            passed = passed + got_side[1, i].astype(F32)
        dq_pair[i] = passed.astype(BF16)
        pair_copy(i, 0).start()

    def finish(i):
        next_own(i).wait_recv()
        dq_out[half * mine + i] = (
            dq_own[i, block(0, half)] + got_far[i, block(0, half)].astype(F32) + got_next[i].astype(F32)
        ).astype(BF16)

    def close(i):
        pair_wait(i, 0)
        side_copy = remote(dq_pair.at[i], got_side.at[0, i], next_send.at[i, 1], side_recv.at[0, i], twin)
        if i == mine - 1:
            side_copy.wait_recv()
        else:
            pl.when(inner)(side_copy.wait_recv)

        dq_out[rest * mine + i] = (got_pair[i].astype(F32) + got_side[0, i].astype(F32)).astype(BF16)

    for a in (2, 3, 0, 1):
        raw_copy(a).wait()
        turn(raws[a], sources[a])
        if a == 2:
            pl.semaphore_wait(barrier, 3 + lax.rem(side + half, 2))
        open_head(0, a)
    for a in (2, 3, 0, 1):
        if mine > 1:
            open_head(1, a)

    @pl.when(outer)
    def _():
        for i in range(mine - 1):
            got_side[:, i] = jnp.zeros((2, tok, depth), BF16)

    for copy in small:
        copy.wait()
    spots = lax.broadcasted_iota(jnp.int32, (1, span), 1) + first_key
    start = jnp.int32(0)
    low = jnp.zeros((1, span), jnp.int32)
    for n in range(doc_ref.shape[0]):
        low = jnp.where(spots >= start, start, low)
        start = start + doc_ref[n]
    low = jnp.where(spots >= start, spots + 1, low)
    low_ref[...] = (low - first_key).astype(F32)

    relay(0)
    if mine > 1:
        relay(1)
    held = []
    for i in range(2, mine):
        for a in (2, 3, 0, 1):
            open_head(i, a)
    for i in range(mine):
        arrived(i)
        gather(i, i % 2)
        for m in held:
            send_next(m)
        held = []
        if i >= 1:
            spread(i - 1, (i - 1) % 2)
            held = [i - 1]
        if i + 2 < mine:
            relay(i + 2)
    for m in held:
        send_next(m)
    spread(mine - 1, (mine - 1) % 2)
    send_next(mine - 1)
    for i in range(mine):
        settle(i)
    for i in range(mine):
        finish(i)

    for a in (1, 2):
        for i in range(mine):
            pair_wait(i, a)
    for i in range(mine):
        close(i)

    for i in range(mine):
        for a in range(4):
            in_copy(i, a).wait_send()
        for a in (2, 3):
            near_own(i, a).wait_send()
            far_copy(i, a).wait_send()
        for m in range(6):
            stat_copy(i, m).wait_send()
        next_own(i).wait_send()
        next_side(i).wait_send()
        back_copy(i).wait_send()
        for a in range(3):
            pair_copy(i, a).wait_send()

    @pl.when(inner)
    def _():
        for i in range(mine):
            for a in (2, 3):
                near_other(i, a).wait_send()
                near_relay(i, a).wait_send()


def chain_call(n_ctx, tok, heads, depth, slots, docs):
    mine = heads // 2
    chunk = 2 * tok
    away = pl.BlockSpec(memory_space=pltpu.MemorySpace.HBM)
    dma = pltpu.SemaphoreType.DMA
    out = jax.ShapeDtypeStruct((heads, tok, depth), BF16)
    near = pl.BlockSpec(memory_space=pltpu.VMEM)
    pairs = mine * 6 * chunk * tok
    return pl.pallas_call(
        partial(chain_kernel, (n_ctx, mine, tok, depth)),
        out_shape=(out, out, out),
        in_specs=[away] * 6,
        out_specs=(near,) * 3,
        scratch_shapes=[pltpu.VMEM((tok, heads, depth), BF16)] * 4
        + [pltpu.VMEM((heads, tok, depth), BF16)] * 4
        + [
            pltpu.SMEM(slots, F32),
            pltpu.SMEM(docs, jnp.int32),
            pltpu.VMEM((1, 3 * chunk), F32),
            pltpu.VMEM((mine, chunk, depth), BF16),
            pltpu.VMEM((mine, chunk, depth), BF16),
            pltpu.VMEM((mine, 3 * chunk, depth), BF16),
            pltpu.VMEM((mine, 3 * chunk, depth), BF16),
            pltpu.VMEM((2, 6, 2, tok, tok), F32),
            pltpu.VMEM((2, 6, 2, tok, tok), F32),
            pltpu.VMEM((2, 6, 1, tok), F32),
            pltpu.VMEM((mine, 3, 4 * tok // depth, depth), F32),
            pltpu.VMEM((mine, 3, 2, 4 * tok // depth, depth), F32),
            pltpu.VMEM((2, 6, 1, tok), F32),
            pltpu.VMEM((depth, tok), F32),
            pltpu.VMEM((chunk, depth), F32),
            pltpu.VMEM((chunk, depth), F32),
            pltpu.VMEM((3 * chunk, depth), F32),
            pltpu.VMEM((mine, chunk, depth), F32),
            pltpu.VMEM((mine, chunk, depth), BF16),
            pltpu.VMEM((mine, chunk, depth), BF16),
            pltpu.VMEM((mine, tok, depth), BF16),
            pltpu.VMEM((mine, chunk, depth), BF16),
            pltpu.VMEM((2, mine, tok, depth), BF16),
            pltpu.VMEM((mine, tok, depth), BF16),
            pltpu.VMEM((mine, tok, depth), BF16),
            pltpu.VMEM((mine, tok, depth), BF16),
            pltpu.VMEM((mine, tok, depth), BF16),
            dma((2,)),
            dma((4,)),
            dma((mine, 4)),
            dma((mine, 4)),
            dma((mine, 4)),
            dma((mine, 2, 3)),
            dma((mine, 2, 2)),
            dma((mine, 2)),
            dma((mine, 2)),
            dma((mine, 6)),
            dma((mine, 3, 2)),
            dma((mine, 2)),
            dma((mine,)),
            dma((2, mine)),
            dma((mine,)),
            dma((mine,)),
            dma((mine, 3)),
            dma((mine, 3)),
        ],
        compiler_params=pltpu.CompilerParams(
            collective_id=1, has_side_effects=True, vmem_limit_bytes=VMEM_PART
        ),
        cost_estimate=pl.CostEstimate(
            flops=10 * pairs * depth, bytes_accessed=14 * heads * tok * depth, transcendentals=pairs
        ),
    )


def turn_over(a_in, b_in, c_in, a_out, b_out, c_out, a_buf, b_buf, c_buf, sem):
    tok = a_buf.shape[0]
    step = min(64, tok)
    copies = []
    for m, (x, buf, y) in enumerate(((b_in, b_buf, b_out), (c_in, c_buf, c_out), (a_in, a_buf, a_out))):
        for n in range(0, tok, step):
            buf[n : n + step] = jnp.swapaxes(x[:, n : n + step], 0, 1)
        copies.append(pltpu.make_async_copy(buf, y, sem.at[m]))
        copies[-1].start()
    for copy in copies:
        copy.wait()


def hand_over(a_in, b_in, c_in, a_out, b_out, c_out, a_buf, b_buf, c_buf, in_sem, out_sem):
    bufs = (a_buf, b_buf, c_buf)
    ins = [pltpu.make_async_copy(x, bufs[n], in_sem.at[n]) for n, x in enumerate((a_in, b_in, c_in))]
    outs = [pltpu.make_async_copy(bufs[n], x, out_sem.at[n]) for n, x in enumerate((a_out, b_out, c_out))]
    for copy in ins:
        copy.start()
    for arrive, leave in zip(ins, outs):
        arrive.wait()
        leave.start()
    for copy in outs:
        copy.wait()


def stay(x):
    return pltpu.with_memory_space_constraint(x, pltpu.MemorySpace.HBM)


def body(queries, keys_in, values, grad_out, slopes, doc_lengths):
    n_head = lax.axis_size("head")
    n_ctx = lax.axis_size("ctx")
    tok, heads, depth = queries.shape
    here = heads // n_head
    rows = tok * n_head
    span = min(16384, rows * n_ctx // 8)
    reach = span // rows
    past = reach * rows
    tile = min(256, rows)
    sizes = (n_head, n_ctx, reach, here, tok, rows, depth, tile)
    away = pl.BlockSpec(memory_space=pl.ANY)
    dma = pltpu.SemaphoreType.DMA
    out = jax.ShapeDtypeStruct((tok, heads, depth), BF16)
    swapped = pltpu.VMEM((heads, tok, depth), BF16)
    window = past + tile
    pairs = rows * window * here
    call = pl.pallas_call(
        partial(kernel, sizes),
        out_shape=(out, out, out),
        in_specs=[away] * 6,
        out_specs=(away,) * 3,
        scratch_shapes=[pltpu.VMEM((tok, heads, depth), BF16)] * 4
        + [swapped] * 7
        + [
            pltpu.SMEM(slopes.shape, F32),
            pltpu.SMEM(doc_lengths.shape, jnp.int32),
            pltpu.VMEM((1, rows), F32),
            pltpu.VMEM((here, past + rows, depth), BF16),
            pltpu.VMEM((here, past + rows, depth), BF16),
            pltpu.VMEM((here, rows, depth), BF16),
            pltpu.VMEM((here, rows, depth), BF16),
            pltpu.VMEM((window, tile), F32),
            pltpu.VMEM((window, tile), F32),
            pltpu.VMEM((1, tile), F32),
            pltpu.VMEM((1, tile), F32),
            pltpu.VMEM((1, tile), F32),
            pltpu.VMEM((depth, tile), F32),
            pltpu.VMEM((past + rows, depth), F32),
            pltpu.VMEM((past + rows, depth), F32),
            pltpu.VMEM((here, rows, depth), BF16),
            pltpu.VMEM((here, rows, depth), BF16),
            pltpu.VMEM((here, rows, depth), BF16),
            pltpu.VMEM((here, past, depth), BF16),
            pltpu.VMEM((here, past, depth), BF16),
            pltpu.VMEM((here, reach, rows, depth), BF16),
            pltpu.VMEM((here, reach, rows, depth), BF16),
            dma((2,)),
            dma((4,)),
            dma((here, 4)),
            dma((here, 4, n_head - 1)),
            dma((here, 4, n_head - 1)),
            dma((here, 2, reach)),
            dma((here, 2, reach)),
            dma((here, 2, reach)),
            dma((here, 2, reach)),
            dma((here, 3, n_head - 1)),
            dma((here, 3, n_head - 1)),
        ],
        compiler_params=pltpu.CompilerParams(
            collective_id=0, has_side_effects=True, vmem_limit_bytes=VMEM_ALL
        ),
        cost_estimate=pl.CostEstimate(
            flops=10 * pairs * depth, bytes_accessed=14 * heads * tok * depth, transcendentals=pairs
        ),
    )
    if n_head == 4 and past == rows and heads % 2 == 0 and tok % (2 * depth) == 0:
        call = chain_call(n_ctx, tok, heads, depth, slopes.shape, doc_lengths.shape)
        near = pl.BlockSpec(memory_space=pltpu.VMEM)
        return pl.pallas_call(
            turn_over,
            out_shape=(out, out, out),
            in_specs=[near] * 3,
            out_specs=(away,) * 3,
            scratch_shapes=[pltpu.VMEM((tok, heads, depth), BF16)] * 3 + [dma((3,))],
            compiler_params=pltpu.CompilerParams(vmem_limit_bytes=VMEM_PART),
        )(*call(*(stay(x) for x in (keys_in, values, queries, grad_out, slopes, doc_lengths))))
    grads = call(keys_in, values, queries, grad_out, slopes, doc_lengths)
    return pl.pallas_call(
        hand_over,
        out_shape=(out, out, out),
        in_specs=[away] * 3,
        out_specs=(away,) * 3,
        scratch_shapes=[pltpu.VMEM((tok, heads, depth), BF16)] * 3 + [dma((3,)), dma((3,))],
        compiler_params=pltpu.CompilerParams(vmem_limit_bytes=VMEM_ALL),
    )(*grads)


def solution(mesh):
    placed = P(("ctx", "head"), None, None)
    return jax.shard_map(
        body,
        mesh=mesh,
        in_specs=(placed, placed, placed, placed, P(), P()),
        out_specs=(placed, placed, placed),
        check_vma=False,
    )
```
